256 devices in a mesh: context: 64 (over y, x_lo, z), heads: 4 (over x_hi, core).
Axes of the slice: x: 4 (x_hi: 2, x_lo: 2; x = x_hi * 2 + x_lo), y: 4, z: 8, core: 2. Of those that a mesh axis runs over, the one named last changes fastest.
Arguments:
- upstream: bfloat16 [16384, 1024], P(('context', 'heads')), may hold values from -48 to 48
- out_weight: bfloat16 [1024, 1024], P('heads'), may hold values from -0.1875 to 0.1875
- query_rows: bfloat16 [16384, 1024], P('context', 'heads'), may hold values from -6 to 6
- key_rows: bfloat16 [16384, 1024], P('context', 'heads'), may hold values from -6 to 6
- value_rows: bfloat16 [16384, 1024], P('context', 'heads'), may hold values from -6 to 6
- head_offsets: int32 [16], replicated, may hold values from 0 to 15, each once
Outputs:
- query_grad: bfloat16 [16384, 1024], P('context', 'heads')
- key_grad: bfloat16 [16384, 1024], P('context', 'heads')
- value_grad: bfloat16 [16384, 1024], P('context', 'heads')
The draws below stay inside these ranges and needn't reach their ends.
Inputs may be any that keep to these rules, and one draw needn't show every extreme that they name: `head_offsets`: every value of 0 to 15 occurs once.
All inputs are finite; a program needn't handle non-finite values.
Results may differ from the reference program's by a relative error of at most 0.008.
Values may be sent and summed in bfloat16 or wider, within the bound.
A program may use at most 128 MiB of HBM per device.

```python
import math
import jax
import jax.numpy as jnp
from jax import lax

D = 1024
H = 16
HEAD_SIZE = 64
DILATION_RATE = 16
FIRST_SEGMENT = 2048
SEQUENCE_TOKENS = 16384
SECOND_SEGMENT = 16384


def draw_query_rows(key, part):
    source = jax.random.fold_in(key, 1)
    value_tensor = jax.random.truncated_normal(source, -6.0, 6.0, (SEQUENCE_TOKENS, D), jnp.float32)
    return value_tensor.astype(jnp.bfloat16)


def draw_key_rows(key, part):
    source = jax.random.fold_in(key, 2)
    value_tensor = jax.random.truncated_normal(source, -6.0, 6.0, (SEQUENCE_TOKENS, D), jnp.float32)
    return value_tensor.astype(jnp.bfloat16)


def steps_of(own_key, shape, split, smallest, top_value):
    loudness, own = 1.0, jax.random.fold_in(own_key, 6)
    for axis_at, blocks in split:
        steps = jnp.exp(jax.random.uniform(jax.random.fold_in(own, axis_at), (blocks,), jnp.float32, smallest / len(split), top_value / len(split)))
        loudness = loudness * jnp.repeat(steps, shape[axis_at] // blocks).reshape([-1 if axis == axis_at else 1 for axis in range(len(shape))])
    return loudness


def bell_draw(stream_key, dims, scale, bound, cuts=(), kind=jnp.bfloat16):
    factor_of = steps_of(stream_key, dims, cuts, -0.22, 0.18) if cuts else 1.0
    entries = jax.random.normal(stream_key, dims, jnp.float32) * scale * factor_of
    return jnp.minimum(jnp.maximum(entries, -bound), bound).astype(kind)


def setup_inputs(seed: int = 0) -> dict:
    streams_of = jax.random.split(jax.random.key(seed), 7)
    return {
        "upstream": jnp.clip(jax.random.uniform(streams_of[0], (SEQUENCE_TOKENS, D), jnp.float32, -48.0, 48.0) * steps_of(streams_of[0], (SEQUENCE_TOKENS, D), ((0, 256),), -0.4, 0.0), -48.0, 48.0).astype(jnp.bfloat16),
        "out_weight": bell_draw(streams_of[1], (D, D), D ** -0.5, 0.1875, ((0, 4),)),
        "query_rows": draw_query_rows(jax.random.fold_in(streams_of[6], 71), 0),
        "key_rows": draw_key_rows(jax.random.fold_in(streams_of[6], 71), 0),
        "value_rows": bell_draw(streams_of[4], (SEQUENCE_TOKENS, D), 1.0, 6.0, ((0, 64), (1, 4))),
        "head_offsets": jax.random.permutation(streams_of[5], H).astype(jnp.int32),
    }


def spread_rows(value_tensor, head_shift):
    total_count = value_tensor.shape[0]
    matched_flag = jnp.arange(DILATION_RATE, dtype=jnp.int32)[None, :] == head_shift
    return jnp.where(matched_flag, value_tensor[:, None], jnp.zeros((), value_tensor.dtype)).reshape(total_count * DILATION_RATE)

def place_rows(value_tensor, head_shift):
    total_count = value_tensor.shape[0]
    matched_flag = (jnp.arange(DILATION_RATE, dtype=jnp.int32) == head_shift)[None, :, None]
    return jnp.where(matched_flag, value_tensor[:, None, :], jnp.zeros((), value_tensor.dtype)).reshape(total_count * DILATION_RATE, value_tensor.shape[1])

def batched(form, left, right):
    return jnp.einsum(form, left.astype(jnp.float32), right.astype(jnp.float32))

def head_grads(query_head, key_head, value_head, grad_head, head_shift):
    scale = 1.0 / math.sqrt(HEAD_SIZE)
    selected_count = SEQUENCE_TOKENS // DILATION_RATE

    def pick(payload_arrays):
        return lax.dynamic_index_in_dim(payload_arrays.reshape(selected_count, DILATION_RATE, HEAD_SIZE), head_shift, 1, keepdims=False)
    query_pick = pick(query_head)
    key_pick = pick(key_head)
    value_pick = pick(value_head)
    grad_pick = pick(grad_head)
    near_segs = SEQUENCE_TOKENS // FIRST_SEGMENT
    local_count = FIRST_SEGMENT // DILATION_RATE
    far_segs = SEQUENCE_TOKENS // SECOND_SEGMENT
    distant_count = SECOND_SEGMENT // DILATION_RATE
    near_keys = key_head.reshape(near_segs, FIRST_SEGMENT, HEAD_SIZE)
    near_values = value_head.reshape(near_segs, FIRST_SEGMENT, HEAD_SIZE)
    score_near = batched('sqd,skd->sqk', query_pick.reshape(near_segs, local_count, HEAD_SIZE), near_keys) * scale
    dprob_near = batched('sqd,skd->sqk', grad_pick.reshape(near_segs, local_count, HEAD_SIZE), near_values)
    score_near = score_near.reshape(selected_count, FIRST_SEGMENT)
    dprob_near = dprob_near.reshape(selected_count, FIRST_SEGMENT)
    query_far = query_pick.reshape(far_segs, distant_count, HEAD_SIZE)
    key_far = key_pick.reshape(far_segs, distant_count, HEAD_SIZE)
    value_far = value_pick.reshape(far_segs, distant_count, HEAD_SIZE)
    grad_far = grad_pick.reshape(far_segs, distant_count, HEAD_SIZE)
    score_far = (batched('sqd,skd->sqk', query_far, key_far) * scale).reshape(selected_count, distant_count)
    dprob_far = batched('sqd,skd->sqk', grad_far, value_far).reshape(selected_count, distant_count)
    row_max = jnp.maximum(lax.optimization_barrier(jnp.max(score_near, 1)), lax.optimization_barrier(jnp.max(score_far, 1)))
    row_sum = lax.optimization_barrier(jnp.sum(jnp.exp(score_near - row_max[:, None]), 1)) + lax.optimization_barrier(jnp.sum(jnp.exp(score_far - row_max[:, None]), 1))
    lse_pick = row_max + jnp.log(row_sum)
    prob_near = jnp.exp(score_near - lse_pick[:, None])
    prob_far = jnp.exp(score_far - lse_pick[:, None])
    delta_pick = lax.optimization_barrier(jnp.sum(prob_near * dprob_near, 1)) + lax.optimization_barrier(jnp.sum(prob_far * dprob_far, 1))
    dscore_far = (prob_far * (dprob_far - delta_pick[:, None])).astype(jnp.bfloat16).reshape(far_segs, distant_count, distant_count)
    prob_far16 = prob_far.astype(jnp.bfloat16).reshape(far_segs, distant_count, distant_count)
    dq_far = (batched('sqk,skd->sqd', dscore_far, key_far) * scale).reshape(selected_count, HEAD_SIZE)
    dk_far = (batched('sqk,sqd->skd', dscore_far, query_far) * scale).reshape(selected_count, HEAD_SIZE)
    dv_far = batched('sqk,sqd->skd', prob_far16, grad_far).reshape(selected_count, HEAD_SIZE)
    lse_rows = spread_rows(lse_pick, head_shift)
    delta_rows = spread_rows(delta_pick, head_shift)
    selected_rows = jnp.arange(SEQUENCE_TOKENS, dtype=jnp.int32) % DILATION_RATE == head_shift

    def segment(inputs):
        seg_query, seg_key, seg_value, seg_grad, seg_lse, seg_delta, seg_mask = inputs
        scores = jnp.dot(seg_query, seg_key.T, preferred_element_type=jnp.float32) * scale
        seg_max = lax.optimization_barrier(jnp.max(scores, 1))
        seg_sum = lax.optimization_barrier(jnp.sum(jnp.exp(scores - seg_max[:, None]), 1))
        lse_all = jnp.where(seg_mask, seg_lse, seg_max + jnp.log(seg_sum))
        probs = jnp.exp(scores - lse_all[:, None])
        dprobs = jnp.dot(seg_grad, seg_value.T, preferred_element_type=jnp.float32)
        delta_all = jnp.where(seg_mask, seg_delta, lax.optimization_barrier(jnp.sum(probs * dprobs, 1)))
        dscores = (probs * (dprobs - delta_all[:, None])).astype(jnp.bfloat16)
        probs16 = probs.astype(jnp.bfloat16)
        dq_seg = jnp.dot(dscores, seg_key, preferred_element_type=jnp.float32) * scale
        dk_seg = jnp.dot(dscores.T, seg_query, preferred_element_type=jnp.float32) * scale
        dv_seg = jnp.dot(probs16.T, seg_grad, preferred_element_type=jnp.float32)
        return (dq_seg, dk_seg, dv_seg)
    dq_near, dk_near, dv_near = lax.map(segment, (query_head.reshape(near_segs, FIRST_SEGMENT, HEAD_SIZE), near_keys, near_values, grad_head.reshape(near_segs, FIRST_SEGMENT, HEAD_SIZE), lse_rows.reshape(near_segs, FIRST_SEGMENT), delta_rows.reshape(near_segs, FIRST_SEGMENT), selected_rows.reshape(near_segs, FIRST_SEGMENT)))
    dq_all = dq_near.reshape(SEQUENCE_TOKENS, HEAD_SIZE) + place_rows(dq_far, head_shift)
    dk_all = dk_near.reshape(SEQUENCE_TOKENS, HEAD_SIZE) + place_rows(dk_far, head_shift)
    dv_all = dv_near.reshape(SEQUENCE_TOKENS, HEAD_SIZE) + place_rows(dv_far, head_shift)
    return (dq_all.astype(jnp.bfloat16), dk_all.astype(jnp.bfloat16), dv_all.astype(jnp.bfloat16))

def reference(upstream, out_weight, query_rows, key_rows, value_rows, head_offsets):
    attn_grad = jnp.dot(upstream, out_weight.T, preferred_element_type=jnp.float32).astype(jnp.bfloat16)

    def one_head(index):

        def columns(payload_arrays):
            return lax.dynamic_slice_in_dim(payload_arrays, index * HEAD_SIZE, HEAD_SIZE, 1)
        return head_grads(columns(query_rows), columns(key_rows), columns(value_rows), columns(attn_grad), head_offsets[index])
    dq_heads, dk_heads, dv_heads = lax.map(one_head, jnp.arange(H, dtype=jnp.int32))

    def merge_heads(payload_arrays):
        return jnp.transpose(payload_arrays, (1, 0, 2)).reshape(SEQUENCE_TOKENS, D)
    return (merge_heads(dq_heads), merge_heads(dk_heads), merge_heads(dv_heads))
```

```python
import functools

import jax
import jax.numpy as jnp
from jax import lax
from jax.experimental import pallas as pl
from jax.experimental.pallas import tpu as pltpu
from jax.sharding import PartitionSpec as P

Z = 8
RATE = 16
BF = jnp.bfloat16
F32 = jnp.float32
MESH = pl.DeviceIdType.MESH
LOW = -1e30


def nn(a, b):
    return lax.dot_general(a, b, (((1,), (0,)), ((), ())), preferred_element_type=F32)


def nt(a, b):
    return lax.dot_general(a, b, (((1,), (1,)), ((), ())), preferred_element_type=F32)


def iota(shape, dim):
    return lax.broadcasted_iota(jnp.int32, shape, dim)


def place(rows, offset, zl):
    return 16 * (((rows & 15) - offset + zl + 16) & 15) + (rows >> 4)


def attn_kernel(
    nseg,
    off_ref, up_ref, w_ref, q_ref, k_ref, v_ref,
    rkv, rq,
    kvs, qts, ots, kv, qt, ot, up, pick, fk, ex, dp,
    m_s, l_s, d_s, f_s, dqt, fse, fre, sse, sre, dkv_s, rks, rqs,
    up_ss, up_rs, qt_ss, qt_rs, kv_ss, kv_rs, fw_ss, ot_ss, ot_rs,
    fa_ss, fa_rs, fb_ss, fb_rs, si_ss, si_rs, rk_ss, rk_rs, rq_ss, rq_rs,
):
    ctx = lax.axis_index("context")
    hd = lax.axis_index("heads")
    s = lax.div(ctx, Z)
    z = lax.rem(ctx, Z)
    xh = lax.div(hd, 2)
    c = lax.rem(hd, 2)
    zh = lax.div(z, 4)
    zl = lax.rem(z, 4)
    oc = 1 - c

    def dev(sv, zv, xv, cv):
        return {"context": sv * Z + zv, "heads": xv * 2 + cv}

    sibling = dev(s, z, xh, oc)
    partner = dev(s, z, 1 - xh, c)

    def peer(i):
        return dev(s, 4 * c + i, xh, zh)

    def far_seg(t):
        return lax.rem(s + t, nseg)

    def is_me(i):
        return jnp.logical_and(zh == c, zl == i)

    def rdma(src, dst, ss, rs, device):
        return pltpu.make_async_remote_copy(
            src_ref=src, dst_ref=dst, send_sem=ss, recv_sem=rs, device_id=device, device_id_type=MESH
        )

    def peer_send(src, dst, ss, rs, i):
        me = is_me(i)

        @pl.when(me)
        def _():
            pltpu.make_async_copy(src, dst, rs).start()

        @pl.when(jnp.logical_not(me))
        def _():
            rdma(src, dst, ss, rs, peer(i)).start()

    def peer_sent(src, ss, i):
        @pl.when(jnp.logical_not(is_me(i)))
        def _():
            rdma(src, src, ss, ss, peer(i)).wait_send()

    def arrived(dst, rs):
        pltpu.make_async_copy(dst, dst, rs).wait()

    bar = pltpu.get_barrier_semaphore()

    def hello(device):
        pl.semaphore_signal(bar, inc=1, device_id=device, device_id_type=MESH)

    for i in range(4):
        @pl.when(jnp.logical_not(is_me(i)))
        def _():
            hello(peer(i))
    hello(sibling)
    hello(partner)
    for t in range(1, nseg):
        for cc in range(2):
            hello(dev(far_seg(t), z, xh, cc))

    for b in range(4):
        qt[b, 64:128, :] = jnp.zeros((64, 256), BF)
        ot[b, 0:64, :] = jnp.zeros((64, 256), BF)
    pad = m_s.shape[0]
    m_s[...] = jnp.full(m_s.shape, LOW, F32)
    l_s[...] = jnp.zeros(l_s.shape, F32)
    d_s[...] = jnp.zeros(d_s.shape, F32)
    row = iota((256, 256), 1)
    col = iota((256, 256), 0)
    low_half = iota((256, 128), 1) < 64
    q_t = q_ref[...].astype(F32).T.astype(BF)
    perms = []
    for h in range(4):
        perm = (col == place(row, off_ref[hd * 4 + h], zl)).astype(F32).astype(BF)
        perms.append(perm)
        qts[h] = (nt(q_t[64 * h : 64 * h + 64, :], perm) * 0.125).astype(BF)
        lanes = slice(128 * (h // 2), 128 * (h // 2) + 128)
        k_h = nn(perm, k_ref[:, lanes])
        v_h = nn(perm, v_ref[:, lanes])
        if h % 2:
            k_h = pltpu.roll(k_h, 64, 1)
        else:
            v_h = pltpu.roll(v_h, 64, 1)
        kvs[h] = jnp.where(low_half, k_h, v_h).astype(BF)
    up[hd] = up_ref[...]

    pl.semaphore_wait(bar, 4 + 2 + 2 * (nseg - 1) - jnp.where(zh == c, 1, 0))

    rdma(up_ref, up.at[hd], up_ss.at[0], up_rs.at[0], partner).start()
    rdma(up_ref, up.at[hd], up_ss.at[1], up_rs.at[1], sibling).start()
    for i in range(4):
        peer_send(qts.at[i], qt.at[zl, 0:64, :], qt_ss.at[i], qt_rs.at[zl], i)
    for i in range(4):
        peer_send(kvs.at[i], kv.at[z], kv_ss.at[i], kv_rs.at[z], i)

    far_hd = (1 - xh) * 2 + c
    arrived(up.at[far_hd], up_rs.at[0])
    rdma(up.at[far_hd], up.at[far_hd], up_ss.at[2], up_rs.at[2], sibling).start()
    arrived(up.at[xh * 2 + oc], up_rs.at[1])
    arrived(up.at[(1 - xh) * 2 + oc], up_rs.at[2])
    a_t = nt(w_ref[...], up[...].reshape(256, up.shape[2])).astype(BF)
    for h in range(4):
        ots[h] = nt(a_t[64 * h : 64 * h + 64, :], perms[h]).astype(BF)
    for i in range(4):
        peer_send(ots.at[i], ot.at[zl, 64:128, :], ot_ss.at[i], ot_rs.at[zl], i)

    for i in range(4):
        arrived(qt.at[i, 0:64, :], qt_rs.at[i])

    def score_block(d):
        keys = kv[d]
        for b in range(4):
            st = nn(keys, qt[b])
            mb = jnp.max(st, axis=0, keepdims=True)
            e = jnp.exp(st - mb)
            ex[d, b] = e
            m_s[pl.ds(d, 1), 256 * b : 256 * b + 256] = mb
            l_s[pl.ds(d, 1), 256 * b : 256 * b + 256] = jnp.sum(e, axis=0, keepdims=True)

    def own_block(i, carry):
        d = 4 * c + lax.rem(zl + i, 4)
        arrived(kv.at[d], kv_rs.at[d])
        rdma(kv.at[d], kv.at[d], fw_ss.at[i], kv_rs.at[d], sibling).start()
        score_block(d)
        return carry

    lax.fori_loop(0, 4, own_block, 0)

    for i in range(4):
        pick[16 * i : 16 * i + 16, :] = kv[4 * c + i, 16 * i : 16 * i + 16, :]
    for t in range(1, nseg):
        for cc in range(2):
            rdma(
                pick, fk.at[s, c], fa_ss.at[t, cc], fa_rs.at[s, c], dev(far_seg(t), z, xh, cc)
            ).start()

    def other_block(i, carry):
        d = 4 * oc + lax.rem(zl + i, 4)
        arrived(kv.at[d], kv_rs.at[d])
        score_block(d)
        return carry

    lax.fori_loop(0, 4, other_block, 0)
    for d in range(Z):
        i = d % 4
        fk[s, d // 4, 16 * i : 16 * i + 16, :] = kv[d, 16 * i : 16 * i + 16, :]

    for i in range(4):
        arrived(ot.at[i, 64:128, :], ot_rs.at[i])

    def dprob_block(d, carry):
        keys = kv[d]
        for b in range(4):
            g = nn(keys, ot[b])
            dp[d, b] = g
            d_s[pl.ds(d, 1), 256 * b : 256 * b + 256] = jnp.sum(ex[d, b] * g, axis=0, keepdims=True)
        return carry

    lax.fori_loop(0, Z, dprob_block, 0)

    lane = iota((1, 128), 1)
    mine = [jnp.logical_and(lane >= 16 * b, lane < 16 * b + 16) for b in range(4)]

    def gather_lanes(parts):
        out = jnp.zeros(parts[0].shape, parts[0].dtype)
        for b in range(4):
            out = jnp.where(mine[b], parts[b], out)
        return out

    q_far = gather_lanes([qt[b, :, 0:128].astype(F32) for b in range(4)]).astype(BF)
    o_far = gather_lanes([ot[b, :, 0:128].astype(F32) for b in range(4)]).astype(BF)
    for t in range(1, nseg):
        for cc in range(2):
            arrived(fk.at[far_seg(t), cc], fa_rs.at[far_seg(t), cc])
    far_keys = fk[...].reshape(nseg * 128, 128)
    st = nn(far_keys, q_far)
    m_far = jnp.max(st, axis=0, keepdims=True)
    e_far = jnp.exp(st - m_far)
    l_far = jnp.sum(e_far, axis=0, keepdims=True)
    g_far = nn(far_keys, o_far)
    d_far = jnp.sum(e_far * g_far, axis=0, keepdims=True)
    for b in range(4):
        lanes = slice(256 * b, 256 * b + 128)
        m_s[Z : Z + 1, lanes] = jnp.where(mine[b], m_far, LOW)
        l_s[Z : Z + 1, lanes] = jnp.where(mine[b], l_far, 0.0)
        d_s[Z : Z + 1, lanes] = jnp.where(mine[b], d_far, 0.0)

    m_all = m_s[...]
    m_row = jnp.max(m_all, axis=0, keepdims=True)
    lse = m_row + jnp.log(jnp.sum(l_s[...] * jnp.exp(m_all - m_row), axis=0, keepdims=True))
    factor = jnp.exp(m_all - lse)
    f_s[0:pad, :] = factor
    delta = jnp.sum(factor * d_s[...], axis=0, keepdims=True)
    f_s[pad : pad + 1, :] = delta

    f_far = gather_lanes([factor[Z : Z + 1, 256 * b : 256 * b + 128] for b in range(4)])
    delta_far = gather_lanes([delta[:, 256 * b : 256 * b + 128] for b in range(4)])
    p_far = e_far * f_far
    ds_far = (p_far * (g_far - delta_far)).astype(BF)
    dkv_far = nt(ds_far, q_far) + nt(p_far.astype(BF), o_far)
    fse[...] = dkv_far.astype(BF).reshape(nseg, 2, 64, 128)
    for t in range(1, nseg):
        for cc in range(2):
            rdma(
                fse.at[far_seg(t), cc], fre.at[s, c], fb_ss.at[t, cc], fb_rs.at[s, c],
                dev(far_seg(t), z, xh, cc),
            ).start()
    rdma(fse.at[s, oc], fre.at[s, c], fb_ss.at[0, 0], fb_rs.at[s, c], sibling).start()
    fre[s, c] = fse[s, c]
    keys_t = far_keys.astype(F32).T[0:64, :].astype(BF)
    dq_far = nn(keys_t, ds_far)
    for b in range(4):
        dqt[b, :, 0:128] = jnp.where(mine[b], dq_far, 0.0)
        dqt[b, :, 128:256] = jnp.zeros((64, 128), F32)

    def grad_block(d):
        kt = kv[d].astype(F32).T[0:64, :].astype(BF)
        acc = jnp.zeros((256, 128), F32)
        for b in range(4):
            lanes = slice(256 * b, 256 * b + 256)
            p = ex[d, b] * f_s[pl.ds(d, 1), lanes]
            ds = (p * (dp[d, b] - f_s[pad : pad + 1, lanes])).astype(BF)
            acc = acc + nt(ds, qt[b]) + nt(p.astype(BF), ot[b])
            dqt[b] = dqt[b] + nn(kt, ds)
        return acc

    def sibling_grads(i, carry):
        sse[i] = grad_block(4 * oc + i).astype(BF)
        rdma(sse.at[i], sre.at[i], si_ss.at[i], si_rs.at[i], sibling).start()
        return carry

    lax.fori_loop(0, 4, sibling_grads, 0)
    for t in range(1, nseg):
        for cc in range(2):
            arrived(fre.at[far_seg(t), cc], fb_rs.at[far_seg(t), cc])
    arrived(fre.at[s, oc], fb_rs.at[s, oc])
    fsum = jnp.zeros((64, 128), F32)
    for t in range(nseg):
        for cc in range(2):
            fsum = fsum + fre[t, cc].astype(F32)
    for i in range(4):
        acc = grad_block(4 * c + i)
        arrived(sre.at[i], si_rs.at[i])
        dkv_s[...] = acc + sre[i].astype(F32)
        rows = slice(16 * i, 16 * i + 16)
        dkv_s[rows, :] = dkv_s[rows, :] + fsum[rows, :]
        rks[i] = dkv_s[...].astype(BF)
        peer_send(rks.at[i], rkv.at[zl], rk_ss.at[i], rk_rs.at[zl], i)
    for i in range(4):
        rqs[i] = (dqt[i] * 0.125).astype(BF)
        peer_send(rqs.at[i], rq.at[zl], rq_ss.at[i], rq_rs.at[zl], i)

    for i in range(4):
        arrived(rkv.at[i], rk_rs.at[i])
        arrived(rq.at[i], rq_rs.at[i])

    rdma(up_ref, up_ref, up_ss.at[0], up_ss.at[0], partner).wait_send()
    rdma(up_ref, up_ref, up_ss.at[1], up_ss.at[1], sibling).wait_send()
    rdma(up_ref, up_ref, up_ss.at[2], up_ss.at[2], sibling).wait_send()
    for i in range(4):
        peer_sent(qts.at[i], qt_ss.at[i], i)
        peer_sent(kvs.at[i], kv_ss.at[i], i)
        peer_sent(ots.at[i], ot_ss.at[i], i)
        peer_sent(rks.at[i], rk_ss.at[i], i)
        peer_sent(rqs.at[i], rq_ss.at[i], i)
        rdma(kvs.at[i], kvs.at[i], fw_ss.at[i], fw_ss.at[i], sibling).wait_send()
        rdma(sse.at[i], sse.at[i], si_ss.at[i], si_ss.at[i], sibling).wait_send()
    for t in range(1, nseg):
        for cc in range(2):
            device = dev(far_seg(t), z, xh, cc)
            rdma(pick, pick, fa_ss.at[t, cc], fa_ss.at[t, cc], device).wait_send()
            rdma(pick, pick, fb_ss.at[t, cc], fb_ss.at[t, cc], device).wait_send()
    rdma(pick, pick, fb_ss.at[0, 0], fb_ss.at[0, 0], sibling).wait_send()


def home_kernel(off_ref, rkv, rq, dq_ref, dk_ref, dv_ref):
    ctx = lax.axis_index("context")
    hd = lax.axis_index("heads")
    zl = lax.rem(ctx, 4)
    row = iota((256, 256), 0)
    col = iota((256, 256), 1)
    low_half = iota((256, 128), 1) < 64
    for pair in range(2):
        lanes = slice(128 * pair, 128 * pair + 128)
        both_q = rq[2 * pair : 2 * pair + 2].reshape(128, 256)
        back, queries = [], []
        for h in (2 * pair, 2 * pair + 1):
            perm = (col == place(row, off_ref[hd * 4 + h], zl)).astype(F32).astype(BF)
            back.append(nn(perm, rkv[h]))
            queries.append(nt(perm, both_q))
        dq_ref[:, lanes] = jnp.where(low_half, queries[0], queries[1]).astype(BF)
        dk_ref[:, lanes] = jnp.where(low_half, back[0], pltpu.roll(back[1], 64, 1)).astype(BF)
        dv_ref[:, lanes] = jnp.where(low_half, pltpu.roll(back[0], 64, 1), back[1]).astype(BF)


def solution(mesh):
    nseg = mesh.shape["context"] // Z
    vmem = pl.BlockSpec(memory_space=pltpu.VMEM)
    smem = pl.BlockSpec(memory_space=pltpu.SMEM)
    dma = pltpu.SemaphoreType.DMA
    nq = 1024

    def body(upstream, out_weight, query_rows, key_rows, value_rows, head_offsets):
        width = upstream.shape[1]
        rkv, rq = pl.pallas_call(
            functools.partial(attn_kernel, nseg),
            out_shape=(
                jax.ShapeDtypeStruct((4, 256, 128), BF),
                jax.ShapeDtypeStruct((4, 64, 256), BF),
            ),
            in_specs=[smem] + [vmem] * 5,
            out_specs=(vmem, vmem),
            scratch_shapes=[
                pltpu.VMEM((4, 256, 128), BF),
                pltpu.VMEM((4, 64, 256), BF),
                pltpu.VMEM((4, 64, 256), BF),
                pltpu.VMEM((Z, 256, 128), BF),
                pltpu.VMEM((4, 128, 256), BF),
                pltpu.VMEM((4, 128, 256), BF),
                pltpu.VMEM((4, 64, width), BF),
                pltpu.VMEM((64, 128), BF),
                pltpu.VMEM((nseg, 2, 64, 128), BF),
                pltpu.VMEM((Z, 4, 256, 256), F32),
                pltpu.VMEM((Z, 4, 256, 256), F32),
                pltpu.VMEM((16, nq), F32),
                pltpu.VMEM((16, nq), F32),
                pltpu.VMEM((16, nq), F32),
                pltpu.VMEM((24, nq), F32),
                pltpu.VMEM((4, 64, 256), F32),
                pltpu.VMEM((nseg, 2, 64, 128), BF),
                pltpu.VMEM((nseg, 2, 64, 128), BF),
                pltpu.VMEM((4, 256, 128), BF),
                pltpu.VMEM((4, 256, 128), BF),
                pltpu.VMEM((256, 128), F32),
                pltpu.VMEM((4, 256, 128), BF),
                pltpu.VMEM((4, 64, 256), BF),
                dma((3,)), dma((3,)),
                dma((4,)), dma((4,)),
                dma((4,)), dma((Z,)), dma((4,)),
                dma((4,)), dma((4,)),
                dma((nseg, 2)), dma((nseg, 2)),
                dma((nseg, 2)), dma((nseg, 2)),
                dma((4,)), dma((4,)),
                dma((4,)), dma((4,)),
                dma((4,)), dma((4,)),
            ],
            compiler_params=pltpu.CompilerParams(
                collective_id=0, has_side_effects=True, vmem_limit_bytes=48 * 1024 * 1024
            ),
            name="attn",
        )(head_offsets, upstream, out_weight, query_rows, key_rows, value_rows)
        block = jax.ShapeDtypeStruct(query_rows.shape, BF)
        return pl.pallas_call(
            home_kernel,
            out_shape=(block, block, block),
            in_specs=[smem, vmem, vmem],
            out_specs=(vmem, vmem, vmem),
            name="home",
        )(head_offsets, rkv, rq)

    return jax.shard_map(
        body,
        mesh=mesh,
        in_specs=(
            P(("context", "heads"), None),
            P("heads", None),
            P("context", "heads"),
            P("context", "heads"),
            P("context", "heads"),
            P(),
        ),
        out_specs=(P("context", "heads"), P("context", "heads"), P("context", "heads")),
        check_vma=False,
    )
```

```python
import functools

import jax
import jax.numpy as jnp
from jax import lax
from jax.experimental import pallas as pl
from jax.experimental.pallas import tpu as pltpu
from jax.sharding import PartitionSpec as P

Z = 8
RATE = 16
BF = jnp.bfloat16
F32 = jnp.float32
MESH = pl.DeviceIdType.MESH
LOW = -1e30


def nn(a, b):
    return lax.dot_general(a, b, (((1,), (0,)), ((), ())), preferred_element_type=F32)


def nt(a, b):
    return lax.dot_general(a, b, (((1,), (1,)), ((), ())), preferred_element_type=F32)


def iota(shape, dim):
    return lax.broadcasted_iota(jnp.int32, shape, dim)


def place(rows, offset, zl):
    return 16 * (((rows & 15) - offset + zl + 16) & 15) + (rows >> 4)


def attn_kernel(
    nseg,
    off_h, up_h, w_h, q_h, k_h, v_h,
    rkv, rq, rf,
    off_ref, w_ref, q_ref, k_ref, v_ref,
    kvs, qts, ots, kv, kt, qt, ot, up, pick, fk, fkt, ex, dp,
    m_s, l_s, f_s, fe, fds, acc_s, fse, fre, sse, sre, rks, rqs, rfs,
    in_s, up_ss, up_rs, qt_ss, qt_rs, kv_ss, kv_rs, fw_ss, ot_ss, ot_rs, pk_ss, pk_rs,
    fa_ss, fa_rs, fb_ss, fb_rs, si_ss, si_rs, rk_ss, rk_rs, rq_ss, rq_rs, rf_ss, rf_rs,
):
    ctx = lax.axis_index("context")
    hd = lax.axis_index("heads")
    s = lax.div(ctx, Z)
    z = lax.rem(ctx, Z)
    xh = lax.div(hd, 2)
    c = lax.rem(hd, 2)
    zh = lax.div(z, 4)
    zl = lax.rem(z, 4)
    oc = 1 - c

    def dev(sv, zv, xv, cv):
        return {"context": sv * Z + zv, "heads": xv * 2 + cv}

    sibling = dev(s, z, xh, oc)
    partner = dev(s, z, 1 - xh, c)

    def peer(i):
        return dev(s, 4 * c + i, xh, zh)

    def far_seg(t):
        return lax.rem(s + t, nseg)

    def is_me(i):
        return jnp.logical_and(zh == c, zl == i)

    def rdma(src, dst, ss, rs, device):
        return pltpu.make_async_remote_copy(
            src_ref=src, dst_ref=dst, send_sem=ss, recv_sem=rs, device_id=device, device_id_type=MESH
        )

    def peer_send(src, dst, ss, rs, i):
        me = is_me(i)

        @pl.when(me)
        def _():
            pltpu.make_async_copy(src, dst, rs).start()

        @pl.when(jnp.logical_not(me))
        def _():
            rdma(src, dst, ss, rs, peer(i)).start()

    def peer_sent(src, ss, i):
        @pl.when(jnp.logical_not(is_me(i)))
        def _():
            rdma(src, src, ss, ss, peer(i)).wait_send()

    def arrived(dst, rs):
        pltpu.make_async_copy(dst, dst, rs).wait()

    def order(j):
        return lax.rem(zl + j, 4)

    bar = pltpu.get_barrier_semaphore()

    def hello(device):
        pl.semaphore_signal(bar, inc=1, device_id=device, device_id_type=MESH)

    for i in range(4):
        @pl.when(jnp.logical_not(is_me(i)))
        def _():
            hello(peer(i))
    hello(sibling)
    hello(partner)
    for t in range(1, nseg):
        for cc in range(2):
            hello(dev(far_seg(t), z, xh, cc))

    loads = [
        pltpu.make_async_copy(a, b, in_s.at[n])
        for n, (a, b) in enumerate(
            ((off_h, off_ref), (q_h, q_ref), (k_h, k_ref), (v_h, v_ref), (up_h, up.at[hd]), (w_h, w_ref))
        )
    ]
    for load in loads:
        load.start()

    for b in range(4):
        qt[b, 64:128, :] = jnp.zeros((64, 256), BF)
        ot[b, 0:64, :] = jnp.zeros((64, 256), BF)
    m_s[...] = jnp.full(m_s.shape, LOW, F32)
    l_s[...] = jnp.zeros(l_s.shape, F32)
    row = iota((256, 256), 1)
    col = iota((256, 256), 0)
    low_half = iota((256, 128), 1) < 64
    lane = iota((1, 128), 1)

    for load in loads[:4]:
        load.wait()
    q_t = q_ref[...].astype(F32).T.astype(BF)
    perms = []
    for h in range(4):
        perm = (col == place(row, off_ref[hd * 4 + h], zl)).astype(F32).astype(BF)
        perms.append(perm)
        qts[h] = (nt(q_t[64 * h : 64 * h + 64, :], perm) * 0.125).astype(BF)
        lanes = slice(128 * (h // 2), 128 * (h // 2) + 128)
        k_p = nn(perm, k_ref[:, lanes])
        v_p = nn(perm, v_ref[:, lanes])
        if h % 2:
            k_p = pltpu.roll(k_p, 64, 1)
        else:
            v_p = pltpu.roll(v_p, 64, 1)
        kvs[h] = jnp.where(low_half, k_p, v_p).astype(BF)
    loads[4].wait()

    pl.semaphore_wait(bar, 4 + 2 + 2 * (nseg - 1) - jnp.where(zh == c, 1, 0))

    picked = pl.ds(pl.multiple_of(16 * zl, 16), 16)
    rdma(up.at[hd], up.at[hd], up_ss.at[0], up_rs.at[0], partner).start()
    rdma(up.at[hd], up.at[hd], up_ss.at[1], up_rs.at[1], sibling).start()
    for j in range(4):
        i = order(j)
        peer_send(kvs.at[i, picked, :], pick.at[picked, :], pk_ss.at[i], pk_rs.at[zl], i)
    for j in range(4):
        i = order(j)
        peer_send(qts.at[i], qt.at[zl, 0:64, :], qt_ss.at[i], qt_rs.at[zl], i)
    for j in range(4):
        i = order(j)
        peer_send(kvs.at[i], kv.at[z], kv_ss.at[i], kv_rs.at[z], i)

    for i in range(4):
        arrived(pick.at[16 * i : 16 * i + 16, :], pk_rs.at[i])
    for t in range(1, nseg):
        for cc in range(2):
            rdma(
                pick, fk.at[s, c], fa_ss.at[t, cc], fa_rs.at[s, c], dev(far_seg(t), z, xh, cc)
            ).start()
    rdma(pick, fk.at[s, c], fa_ss.at[0, 0], fa_rs.at[s, c], sibling).start()
    fk[s, c] = pick[...]

    far_hd = (1 - xh) * 2 + c
    arrived(up.at[far_hd], up_rs.at[0])
    rdma(up.at[far_hd], up.at[far_hd], up_ss.at[2], up_rs.at[2], sibling).start()
    arrived(up.at[xh * 2 + oc], up_rs.at[1])
    loads[5].wait()
    arrived(up.at[(1 - xh) * 2 + oc], up_rs.at[2])
    a_t = nt(w_ref[...], up[...].reshape(256, up.shape[2])).astype(BF)
    for h in range(4):
        ots[h] = nt(a_t[64 * h : 64 * h + 64, :], perms[h]).astype(BF)
    for j in range(4):
        i = order(j)
        peer_send(ots.at[i], ot.at[zl, 64:128, :], ot_ss.at[i], ot_rs.at[zl], i)

    for i in range(4):
        arrived(qt.at[i, 0:64, :], qt_rs.at[i])

    def score_block(d):
        keys = kv[d]
        kt[d] = keys.astype(F32).T[0:64, :].astype(BF)
        for b in range(4):
            st = nn(keys, qt[b])
            mb = jnp.max(st, axis=0, keepdims=True)
            e = jnp.exp(st - mb)
            ex[d, b] = e
            m_s[b, pl.ds(d, 1), :] = mb
            l_s[b, pl.ds(d, 1), :] = jnp.sum(e, axis=0, keepdims=True)

    def own_block(j, carry):
        i = lax.rem(zl + 4 - j, 4)
        d = 4 * c + i
        arrived(kv.at[d], kv_rs.at[d])
        rdma(kv.at[d], kv.at[d], fw_ss.at[i], kv_rs.at[d], sibling).start()
        score_block(d)
        return carry

    def other_block(j, carry):
        d = 4 * oc + lax.rem(zl + 4 - j, 4)
        arrived(kv.at[d], kv_rs.at[d])
        score_block(d)
        return carry

    lax.fori_loop(0, 4, own_block, 0)
    lax.fori_loop(0, 4, other_block, 0)

    def mine(b):
        return jnp.logical_and(lane >= 16 * b, lane < 16 * b + 16)

    def gather_lanes(parts):
        out = jnp.zeros(parts[0].shape, parts[0].dtype)
        for b in range(4):
            out = jnp.where(mine(b), parts[b], out)
        return out

    q_far = gather_lanes([qt[b, :, 0:128].astype(F32) for b in range(4)]).astype(BF)
    for t in range(1, nseg):
        for cc in range(2):
            arrived(fk.at[far_seg(t), cc], fa_rs.at[far_seg(t), cc])
    arrived(fk.at[s, oc], fa_rs.at[s, oc])
    far_keys = fk[...].reshape(nseg * 128, 128)
    fkt[...] = far_keys.astype(F32).T[0:64, :].astype(BF)
    st = nn(far_keys, q_far)
    m_far = jnp.max(st, axis=0, keepdims=True)
    e_far = jnp.exp(st - m_far)
    fe[...] = e_far
    l_far = jnp.sum(e_far, axis=0, keepdims=True)
    for b in range(4):
        m_s[b, Z : Z + 1, 0:128] = jnp.where(mine(b), m_far, LOW)
        l_s[b, Z : Z + 1, 0:128] = jnp.where(mine(b), l_far, 0.0)
    for b in range(4):
        m_all = m_s[b]
        m_row = jnp.max(m_all, axis=0, keepdims=True)
        lse = m_row + jnp.log(jnp.sum(l_s[b] * jnp.exp(m_all - m_row), axis=0, keepdims=True))
        f_s[b] = jnp.exp(m_all - lse)
    fe[...] = fe[...] * gather_lanes([f_s[b, Z : Z + 1, 0:128] for b in range(4)])

    for b in range(4):
        arrived(ot.at[b, 64:128, :], ot_rs.at[b])
    o_far = gather_lanes([ot[b, :, 0:128].astype(F32) for b in range(4)]).astype(BF)
    g_far = nn(fk[...].reshape(nseg * 128, 128), o_far)
    fds[...] = g_far
    far_delta = jnp.sum(fe[...] * g_far, axis=0, keepdims=True)

    def dprob_block(d, total):
        keys = kv[d]
        out = []
        for b in range(4):
            g = nn(keys, ot[b])
            dp[d, b] = g
            part = jnp.sum(ex[d, b] * g, axis=0, keepdims=True)
            out.append(total[b] + f_s[b, pl.ds(d, 1), :] * part)
        return tuple(out)

    delta = lax.fori_loop(0, Z, dprob_block, tuple(jnp.zeros((1, 256), F32) for _ in range(4)))
    zero_row = jnp.zeros((1, 128), F32)
    delta = [
        delta[b] + jnp.concatenate([jnp.where(mine(b), far_delta, 0.0), zero_row], axis=1)
        for b in range(4)
    ]
    for b in range(4):
        l_s[b, 0:1, :] = delta[b]

    p_far = fe[...]
    ds_far = (p_far * (fds[...] - gather_lanes([delta[b][:, 0:128] for b in range(4)]))).astype(BF)
    dkv_far = nt(ds_far, q_far) + nt(p_far.astype(BF), o_far)
    fse[...] = dkv_far.astype(BF).reshape(nseg, 2, 64, 128)
    for t in range(1, nseg):
        for cc in range(2):
            rdma(
                fse.at[far_seg(t), cc], fre.at[s, c], fb_ss.at[t, cc], fb_rs.at[s, c],
                dev(far_seg(t), z, xh, cc),
            ).start()
    rdma(fse.at[s, oc], fre.at[s, c], fb_ss.at[0, 0], fb_rs.at[s, c], sibling).start()
    fre[s, c] = fse[s, c]
    dq_far = nn(fkt[...], ds_far)
    for b in range(4):
        acc_s[b, :, 0:128] = jnp.where(mine(b), dq_far, 0.0)
        acc_s[b, :, 128:256] = jnp.zeros((64, 128), F32)

    def grad_block(d):
        grads = jnp.zeros((256, 128), F32)
        keys_t = kt[d]
        for b in range(4):
            p = ex[d, b] * f_s[b, pl.ds(d, 1), :]
            ds = (p * (dp[d, b] - l_s[b, 0:1, :])).astype(BF)
            grads = grads + nt(ds, qt[b]) + nt(p.astype(BF), ot[b])
            acc_s[b] = acc_s[b] + nn(keys_t, ds)
        return grads

    def pair_block(n, carry):
        i = lax.rem(zl + n, 4)
        sse[i] = grad_block(4 * oc + i).astype(BF)
        rdma(sse.at[i], sre.at[i], si_ss.at[i], si_rs.at[i], sibling).start()
        grads = grad_block(4 * c + i)
        arrived(sre.at[i], si_rs.at[i])
        rks[i] = (grads + sre[i].astype(F32)).astype(BF)
        peer_send(rks.at[i], rkv.at[zl], rk_ss.at[i], rk_rs.at[zl], i)
        return carry

    lax.fori_loop(0, 4, pair_block, 0)
    for j in range(4):
        b = order(j)
        rqs[b] = (acc_s[b] * 0.125).astype(BF)
        peer_send(rqs.at[b], rq.at[zl], rq_ss.at[b], rq_rs.at[zl], b)

    for t in range(1, nseg):
        for cc in range(2):
            arrived(fre.at[far_seg(t), cc], fb_rs.at[far_seg(t), cc])
    arrived(fre.at[s, oc], fb_rs.at[s, oc])
    fsum = jnp.zeros((64, 128), F32)
    for t in range(nseg):
        for cc in range(2):
            fsum = fsum + fre[t, cc].astype(F32)
    for i in range(4):
        rfs[i] = fsum[16 * i : 16 * i + 16, :]
    for j in range(4):
        i = order(j)
        peer_send(rfs.at[i], rf.at[zl], rf_ss.at[i], rf_rs.at[zl], i)

    for i in range(4):
        arrived(rkv.at[i], rk_rs.at[i])
        arrived(rq.at[i], rq_rs.at[i])
        arrived(rf.at[i], rf_rs.at[i])

    for n, device in ((0, partner), (1, sibling), (2, sibling)):
        rdma(up.at[0], up.at[0], up_ss.at[n], up_ss.at[n], device).wait_send()
    for i in range(4):
        peer_sent(kvs.at[i, 0:16, :], pk_ss.at[i], i)
        peer_sent(qts.at[i], qt_ss.at[i], i)
        peer_sent(kvs.at[i], kv_ss.at[i], i)
        peer_sent(ots.at[i], ot_ss.at[i], i)
        peer_sent(rks.at[i], rk_ss.at[i], i)
        peer_sent(rqs.at[i], rq_ss.at[i], i)
        peer_sent(rfs.at[i], rf_ss.at[i], i)
        rdma(kvs.at[i], kvs.at[i], fw_ss.at[i], fw_ss.at[i], sibling).wait_send()
        rdma(sse.at[i], sse.at[i], si_ss.at[i], si_ss.at[i], sibling).wait_send()
    for t in range(1, nseg):
        for cc in range(2):
            device = dev(far_seg(t), z, xh, cc)
            rdma(pick, pick, fa_ss.at[t, cc], fa_ss.at[t, cc], device).wait_send()
            rdma(pick, pick, fb_ss.at[t, cc], fb_ss.at[t, cc], device).wait_send()
    rdma(pick, pick, fa_ss.at[0, 0], fa_ss.at[0, 0], sibling).wait_send()
    rdma(pick, pick, fb_ss.at[0, 0], fb_ss.at[0, 0], sibling).wait_send()


def home_kernel(off_ref, rkv, rq, rf, dq_ref, dk_ref, dv_ref, sums):
    ctx = lax.axis_index("context")
    hd = lax.axis_index("heads")
    zl = lax.rem(ctx, 4)
    row = iota((256, 256), 0)
    col = iota((256, 256), 1)
    low_half = iota((256, 128), 1) < 64
    picked = pl.ds(pl.multiple_of(16 * zl, 16), 16)
    for h in range(4):
        sums[h] = rkv[h].astype(F32)
        sums[h, picked, :] = sums[h, picked, :] + rf[h]
    for pair in range(2):
        lanes = slice(128 * pair, 128 * pair + 128)
        both_q = rq[2 * pair : 2 * pair + 2].reshape(128, 256)
        back, queries = [], []
        for h in (2 * pair, 2 * pair + 1):
            perm = (col == place(row, off_ref[hd * 4 + h], zl)).astype(F32).astype(BF)
            back.append(nn(perm, sums[h].astype(BF)))
            queries.append(nt(perm, both_q))
        dq_ref[:, lanes] = jnp.where(low_half, queries[0], queries[1]).astype(BF)
        dk_ref[:, lanes] = jnp.where(low_half, back[0], pltpu.roll(back[1], 64, 1)).astype(BF)
        dv_ref[:, lanes] = jnp.where(low_half, pltpu.roll(back[0], 64, 1), back[1]).astype(BF)


def solution(mesh):
    nseg = mesh.shape["context"] // Z
    vmem = pl.BlockSpec(memory_space=pltpu.VMEM)
    smem = pl.BlockSpec(memory_space=pltpu.SMEM)
    hbm = pl.BlockSpec(memory_space=pltpu.HBM)
    dma = pltpu.SemaphoreType.DMA

    def body(upstream, out_weight, query_rows, key_rows, value_rows, head_offsets):
        width = upstream.shape[1]
        rkv, rq, rf = pl.pallas_call(
            functools.partial(attn_kernel, nseg),
            out_shape=(
                jax.ShapeDtypeStruct((4, 256, 128), BF),
                jax.ShapeDtypeStruct((4, 64, 256), BF),
                jax.ShapeDtypeStruct((4, 16, 128), F32),
            ),
            in_specs=[hbm] * 6,
            out_specs=(vmem, vmem, vmem),
            scratch_shapes=[
                pltpu.SMEM((16,), jnp.int32),
                pltpu.VMEM(out_weight.shape, BF),
                pltpu.VMEM(query_rows.shape, BF),
                pltpu.VMEM(key_rows.shape, BF),
                pltpu.VMEM(value_rows.shape, BF),
                pltpu.VMEM((4, 256, 128), BF),
                pltpu.VMEM((4, 64, 256), BF),
                pltpu.VMEM((4, 64, 256), BF),
                pltpu.VMEM((Z, 256, 128), BF),
                pltpu.VMEM((Z, 64, 256), BF),
                pltpu.VMEM((4, 128, 256), BF),
                pltpu.VMEM((4, 128, 256), BF),
                pltpu.VMEM((4, 64, width), BF),
                pltpu.VMEM((64, 128), BF),
                pltpu.VMEM((nseg, 2, 64, 128), BF),
                pltpu.VMEM((64, nseg * 128), BF),
                pltpu.VMEM((Z, 4, 256, 256), F32),
                pltpu.VMEM((Z, 4, 256, 256), F32),
                pltpu.VMEM((4, 16, 256), F32),
                pltpu.VMEM((4, 16, 256), F32),
                pltpu.VMEM((4, 16, 256), F32),
                pltpu.VMEM((nseg * 128, 128), F32),
                pltpu.VMEM((nseg * 128, 128), F32),
                pltpu.VMEM((4, 64, 256), F32),
                pltpu.VMEM((nseg, 2, 64, 128), BF),
                pltpu.VMEM((nseg, 2, 64, 128), BF),
                pltpu.VMEM((4, 256, 128), BF),
                pltpu.VMEM((4, 256, 128), BF),
                pltpu.VMEM((4, 256, 128), BF),
                pltpu.VMEM((4, 64, 256), BF),
                pltpu.VMEM((4, 16, 128), F32),
                dma((6,)),
                dma((3,)), dma((3,)),
                dma((4,)), dma((4,)),
                dma((4,)), dma((Z,)), dma((4,)),
                dma((4,)), dma((4,)),
                dma((4,)), dma((4,)),
                dma((nseg, 2)), dma((nseg, 2)),
                dma((nseg, 2)), dma((nseg, 2)),
                dma((4,)), dma((4,)),
                dma((4,)), dma((4,)),
                dma((4,)), dma((4,)),
                dma((4,)), dma((4,)),
            ],
            compiler_params=pltpu.CompilerParams(
                collective_id=0, has_side_effects=True, vmem_limit_bytes=66400000
            ),
            name="attn",
        )(head_offsets, upstream, out_weight, query_rows, key_rows, value_rows)
        block = jax.ShapeDtypeStruct(query_rows.shape, BF)
        return pl.pallas_call(
            home_kernel,
            out_shape=(block, block, block),
            in_specs=[smem, vmem, vmem, vmem],
            out_specs=(vmem, vmem, vmem),
            scratch_shapes=[pltpu.VMEM((4, 256, 128), F32)],
            name="home",
        )(head_offsets, rkv, rq, rf)

    return jax.shard_map(
        body,
        mesh=mesh,
        in_specs=(
            P(("context", "heads"), None),
            P("heads", None),
            P("context", "heads"),
            P("context", "heads"),
            P("context", "heads"),
            P(),
        ),
        out_specs=(P("context", "heads"), P("context", "heads"), P("context", "heads")),
        check_vma=False,
    )
```

```python
import functools

import jax
import jax.numpy as jnp
from jax import lax
from jax.experimental import pallas as pl
from jax.experimental.pallas import tpu as pltpu
from jax.sharding import PartitionSpec as P

Z = 8
RATE = 16
BF = jnp.bfloat16
F32 = jnp.float32
MESH = pl.DeviceIdType.MESH
LOW = -1e30


def nn(a, b):
    return lax.dot_general(a, b, (((1,), (0,)), ((), ())), preferred_element_type=F32)


def nt(a, b):
    return lax.dot_general(a, b, (((1,), (1,)), ((), ())), preferred_element_type=F32)


def iota(shape, dim):
    return lax.broadcasted_iota(jnp.int32, shape, dim)


def place(rows, offset, zl):
    return 16 * (((rows & 15) - offset + zl + 16) & 15) + (rows >> 4)


def origin(places, offset, zl):
    return 16 * (places & 15) + (((places >> 4) + offset - zl + 16) & 15)


def attn_kernel(
    nseg,
    off_h, up_h, w_h, q_h, k_h, v_h,
    rkv, rq, rf,
    off_ref, w_ref, q_ref, k_ref, v_ref,
    kvs, qts, ots, kv, kt, qt, ot, up, pick, fk, fkt, ex, dp,
    m_s, l_s, f_s, fe, fds, acc_s, fse, fre, sse, sre, rks, rqs, rfs,
    in_s, up_ss, up_rs, qt_ss, qt_rs, kv_ss, kv_rs, fw_ss, ot_ss, ot_rs, pk_ss, pk_rs,
    fa_ss, fa_rs, fb_ss, fb_rs, si_ss, si_rs, rk_ss, rk_rs, rq_ss, rq_rs, rf_ss, rf_rs,
):
    ctx = lax.axis_index("context")
    hd = lax.axis_index("heads")
    s = lax.div(ctx, Z)
    z = lax.rem(ctx, Z)
    xh = lax.div(hd, 2)
    c = lax.rem(hd, 2)
    zh = lax.div(z, 4)
    zl = lax.rem(z, 4)
    oc = 1 - c

    def dev(sv, zv, xv, cv):
        return {"context": sv * Z + zv, "heads": xv * 2 + cv}

    sibling = dev(s, z, xh, oc)
    partner = dev(s, z, 1 - xh, c)

    def peer(i):
        return dev(s, 4 * c + i, xh, zh)

    def far_seg(t):
        return lax.rem(s + t, nseg)

    def is_me(i):
        return jnp.logical_and(zh == c, zl == i)

    def rdma(src, dst, ss, rs, device):
        return pltpu.make_async_remote_copy(
            src_ref=src, dst_ref=dst, send_sem=ss, recv_sem=rs, device_id=device, device_id_type=MESH
        )

    def peer_send(src, dst, ss, rs, i):
        me = is_me(i)

        @pl.when(me)
        def _():
            pltpu.make_async_copy(src, dst, rs).start()

        @pl.when(jnp.logical_not(me))
        def _():
            rdma(src, dst, ss, rs, peer(i)).start()

    def peer_sent(src, ss, i):
        @pl.when(jnp.logical_not(is_me(i)))
        def _():
            rdma(src, src, ss, ss, peer(i)).wait_send()

    def arrived(dst, rs):
        pltpu.make_async_copy(dst, dst, rs).wait()

    def order(j):
        return lax.rem(zl + j, 4)

    bar = pltpu.get_barrier_semaphore()

    def hello(device):
        pl.semaphore_signal(bar, inc=1, device_id=device, device_id_type=MESH)

    for i in range(4):
        @pl.when(jnp.logical_not(is_me(i)))
        def _():
            hello(peer(i))
    hello(sibling)
    hello(partner)
    for t in range(1, nseg):
        for cc in range(2):
            hello(dev(far_seg(t), z, xh, cc))

    loads = [
        pltpu.make_async_copy(a, b, in_s.at[n])
        for n, (a, b) in enumerate(
            ((off_h, off_ref), (q_h, q_ref), (k_h, k_ref), (v_h, v_ref), (up_h, up.at[hd]), (w_h, w_ref))
        )
    ]
    for load in loads:
        load.start()

    for b in range(4):
        qt[b, 64:128, :] = jnp.zeros((64, 256), BF)
        ot[b, 0:64, :] = jnp.zeros((64, 256), BF)
    m_s[...] = jnp.full(m_s.shape, LOW, F32)
    l_s[...] = jnp.zeros(l_s.shape, F32)
    row = iota((1, 256), 1)
    col = iota((256, 256), 0)
    low_half = iota((256, 128), 1) < 64
    lane = iota((1, 128), 1)

    for load in loads[:4]:
        load.wait()
    q_t = q_ref[...].astype(F32).T.astype(BF)
    k_v = [
        jnp.concatenate([k_ref[:, n : n + 128], v_ref[:, n : n + 128]], axis=1) for n in (0, 128)
    ]
    perms = []
    for h in range(4):
        perm = (col == place(row, off_ref[hd * 4 + h], zl)).astype(F32).astype(BF)
        perms.append(perm)
        qts[h] = (nt(q_t[64 * h : 64 * h + 64, :], perm) * 0.125).astype(BF)
        both = nn(perm, k_v[h // 2])
        k_p = both[:, 0:128]
        v_p = both[:, 128:256]
        if h % 2:
            k_p = pltpu.roll(k_p, 64, 1)
        else:
            v_p = pltpu.roll(v_p, 64, 1)
        kvs[h] = jnp.where(low_half, k_p, v_p).astype(BF)
    loads[4].wait()

    pl.semaphore_wait(bar, 4 + 2 + 2 * (nseg - 1) - jnp.where(zh == c, 1, 0))

    picked = pl.ds(pl.multiple_of(16 * zl, 16), 16)
    rdma(up.at[hd], up.at[hd], up_ss.at[0], up_rs.at[0], partner).start()
    rdma(up.at[hd], up.at[hd], up_ss.at[1], up_rs.at[1], sibling).start()
    for j in range(4):
        i = order(j)
        peer_send(kvs.at[i, picked, :], pick.at[picked, :], pk_ss.at[i], pk_rs.at[zl], i)
    for j in range(4):
        i = order(j)
        peer_send(qts.at[i], qt.at[zl, 0:64, :], qt_ss.at[i], qt_rs.at[zl], i)
    for j in range(4):
        i = order(j)
        peer_send(kvs.at[i], kv.at[z], kv_ss.at[i], kv_rs.at[z], i)

    for i in range(4):
        arrived(pick.at[16 * i : 16 * i + 16, :], pk_rs.at[i])
    for t in range(1, nseg):
        for cc in range(2):
            rdma(
                pick, fk.at[s, c], fa_ss.at[t, cc], fa_rs.at[s, c], dev(far_seg(t), z, xh, cc)
            ).start()
    rdma(pick, fk.at[s, c], fa_ss.at[0, 0], fa_rs.at[s, c], sibling).start()
    fk[s, c] = pick[...]

    far_hd = (1 - xh) * 2 + c
    arrived(up.at[far_hd], up_rs.at[0])
    rdma(up.at[far_hd], up.at[far_hd], up_ss.at[2], up_rs.at[2], sibling).start()
    arrived(up.at[xh * 2 + oc], up_rs.at[1])
    loads[5].wait()
    arrived(up.at[(1 - xh) * 2 + oc], up_rs.at[2])
    a_t = nt(w_ref[...], up[...].reshape(256, up.shape[2])).astype(BF)
    for h in range(4):
        ots[h] = nt(a_t[64 * h : 64 * h + 64, :], perms[h]).astype(BF)
    for j in range(4):
        i = order(j)
        peer_send(ots.at[i], ot.at[zl, 64:128, :], ot_ss.at[i], ot_rs.at[zl], i)

    for i in range(4):
        arrived(qt.at[i, 0:64, :], qt_rs.at[i])

    def score_block(d):
        keys = kv[d]
        kt[d] = keys.astype(F32).T[0:64, :].astype(BF)
        for b in range(4):
            st = nn(keys, qt[b])
            mb = jnp.max(st, axis=0, keepdims=True)
            e = jnp.exp(st - mb)
            ex[d, b] = e
            m_s[b, pl.ds(d, 1), :] = mb
            l_s[b, pl.ds(d, 1), :] = jnp.sum(e, axis=0, keepdims=True)

    def own_block(j, carry):
        i = lax.rem(zl + 4 - j, 4)
        d = 4 * c + i
        arrived(kv.at[d], kv_rs.at[d])
        rdma(kv.at[d], kv.at[d], fw_ss.at[i], kv_rs.at[d], sibling).start()
        score_block(d)
        return carry

    def other_block(j, carry):
        d = 4 * oc + lax.rem(zl + 4 - j, 4)
        arrived(kv.at[d], kv_rs.at[d])
        score_block(d)
        return carry

    lax.fori_loop(0, 4, own_block, 0)
    lax.fori_loop(0, 4, other_block, 0)

    def mine(b):
        return jnp.logical_and(lane >= 16 * b, lane < 16 * b + 16)

    def gather_lanes(parts):
        out = jnp.zeros(parts[0].shape, parts[0].dtype)
        for b in range(4):
            out = jnp.where(mine(b), parts[b], out)
        return out

    q_far = gather_lanes([qt[b, :, 0:128].astype(F32) for b in range(4)]).astype(BF)
    for t in range(1, nseg):
        for cc in range(2):
            arrived(fk.at[far_seg(t), cc], fa_rs.at[far_seg(t), cc])
    arrived(fk.at[s, oc], fa_rs.at[s, oc])
    far_keys = fk[...].reshape(nseg * 128, 128)
    fkt[...] = far_keys.astype(F32).T[0:64, :].astype(BF)
    st = nn(far_keys, q_far)
    m_far = jnp.max(st, axis=0, keepdims=True)
    e_far = jnp.exp(st - m_far)
    fe[...] = e_far
    l_far = jnp.sum(e_far, axis=0, keepdims=True)
    for b in range(4):
        m_s[b, Z : Z + 1, 0:128] = jnp.where(mine(b), m_far, LOW)
        l_s[b, Z : Z + 1, 0:128] = jnp.where(mine(b), l_far, 0.0)
    for b in range(4):
        m_all = m_s[b]
        m_row = jnp.max(m_all, axis=0, keepdims=True)
        lse = m_row + jnp.log(jnp.sum(l_s[b] * jnp.exp(m_all - m_row), axis=0, keepdims=True))
        f_s[b] = jnp.exp(m_all - lse)
    fe[...] = fe[...] * gather_lanes([f_s[b, Z : Z + 1, 0:128] for b in range(4)])

    for b in range(4):
        arrived(ot.at[b, 64:128, :], ot_rs.at[b])
    o_far = gather_lanes([ot[b, :, 0:128].astype(F32) for b in range(4)]).astype(BF)
    g_far = nn(fk[...].reshape(nseg * 128, 128), o_far)
    fds[...] = g_far
    far_delta = jnp.sum(fe[...] * g_far, axis=0, keepdims=True)

    def dprob_block(d, total):
        keys = kv[d]
        out = []
        for b in range(4):
            g = nn(keys, ot[b])
            dp[d, b] = g
            part = jnp.sum(ex[d, b] * g, axis=0, keepdims=True)
            out.append(total[b] + f_s[b, pl.ds(d, 1), :] * part)
        return tuple(out)

    delta = lax.fori_loop(0, Z, dprob_block, tuple(jnp.zeros((1, 256), F32) for _ in range(4)))
    zero_row = jnp.zeros((1, 128), F32)
    delta = [
        delta[b] + jnp.concatenate([jnp.where(mine(b), far_delta, 0.0), zero_row], axis=1)
        for b in range(4)
    ]
    for b in range(4):
        l_s[b, 0:1, :] = delta[b]

    p_far = fe[...]
    ds_far = (p_far * (fds[...] - gather_lanes([delta[b][:, 0:128] for b in range(4)]))).astype(BF)
    dkv_far = nt(ds_far, q_far) + nt(p_far.astype(BF), o_far)
    fse[...] = dkv_far.astype(BF).reshape(nseg, 2, 64, 128)
    for t in range(1, nseg):
        for cc in range(2):
            rdma(
                fse.at[far_seg(t), cc], fre.at[s, c], fb_ss.at[t, cc], fb_rs.at[s, c],
                dev(far_seg(t), z, xh, cc),
            ).start()
    rdma(fse.at[s, oc], fre.at[s, c], fb_ss.at[0, 0], fb_rs.at[s, c], sibling).start()
    fre[s, c] = fse[s, c]
    dq_far = nn(fkt[...], ds_far)
    for b in range(4):
        acc_s[b, :, 0:128] = jnp.where(mine(b), dq_far, 0.0)
        acc_s[b, :, 128:256] = jnp.zeros((64, 128), F32)

    def grad_block(d):
        key_grads = jnp.zeros((64, 256), F32)
        value_grads = jnp.zeros((64, 256), F32)
        keys_t = kt[d]
        for b in range(4):
            p = ex[d, b] * f_s[b, pl.ds(d, 1), :]
            ds = (p * (dp[d, b] - l_s[b, 0:1, :])).astype(BF)
            key_grads = key_grads + nt(qt[b, 0:64, :], ds)
            value_grads = value_grads + nt(ot[b, 64:128, :], p.astype(BF))
            acc_s[b] = acc_s[b] + nn(keys_t, ds)
        return jnp.concatenate([key_grads, value_grads], axis=0)

    def pair_block(n, carry):
        i = lax.rem(zl + n, 4)
        sse[i] = grad_block(4 * oc + i).astype(BF)
        rdma(sse.at[i], sre.at[i], si_ss.at[i], si_rs.at[i], sibling).start()
        grads = grad_block(4 * c + i)
        arrived(sre.at[i], si_rs.at[i])
        rks[i] = (grads + sre[i].astype(F32)).astype(BF)
        peer_send(rks.at[i], rkv.at[zl], rk_ss.at[i], rk_rs.at[zl], i)
        return carry

    lax.fori_loop(0, 4, pair_block, 0)
    for j in range(4):
        b = order(j)
        rqs[b] = (acc_s[b] * 0.125).astype(BF)
        peer_send(rqs.at[b], rq.at[zl], rq_ss.at[b], rq_rs.at[zl], b)

    for t in range(1, nseg):
        for cc in range(2):
            arrived(fre.at[far_seg(t), cc], fb_rs.at[far_seg(t), cc])
    arrived(fre.at[s, oc], fb_rs.at[s, oc])
    fsum = jnp.zeros((64, 128), F32)
    for t in range(nseg):
        for cc in range(2):
            fsum = fsum + fre[t, cc].astype(F32)
    for i in range(4):
        rfs[i] = fsum[16 * i : 16 * i + 16, :]
    for j in range(4):
        i = order(j)
        peer_send(rfs.at[i], rf.at[zl], rf_ss.at[i], rf_rs.at[zl], i)

    for n, device in ((0, partner), (1, sibling), (2, sibling)):
        rdma(up.at[0], up.at[0], up_ss.at[n], up_ss.at[n], device).wait_send()
    for i in range(4):
        peer_sent(kvs.at[i, 0:16, :], pk_ss.at[i], i)
        peer_sent(qts.at[i], qt_ss.at[i], i)
        peer_sent(kvs.at[i], kv_ss.at[i], i)
        peer_sent(ots.at[i], ot_ss.at[i], i)
        peer_sent(rks.at[i], rk_ss.at[i], i)
        peer_sent(rqs.at[i], rq_ss.at[i], i)
        peer_sent(rfs.at[i], rf_ss.at[i], i)
        rdma(kvs.at[i], kvs.at[i], fw_ss.at[i], fw_ss.at[i], sibling).wait_send()
        rdma(sse.at[i], sse.at[i], si_ss.at[i], si_ss.at[i], sibling).wait_send()
    for t in range(1, nseg):
        for cc in range(2):
            device = dev(far_seg(t), z, xh, cc)
            rdma(pick, pick, fa_ss.at[t, cc], fa_ss.at[t, cc], device).wait_send()
            rdma(pick, pick, fb_ss.at[t, cc], fb_ss.at[t, cc], device).wait_send()
    rdma(pick, pick, fa_ss.at[0, 0], fa_ss.at[0, 0], sibling).wait_send()
    rdma(pick, pick, fb_ss.at[0, 0], fb_ss.at[0, 0], sibling).wait_send()

    for i in range(4):
        arrived(rkv.at[i], rk_rs.at[i])
        arrived(rq.at[i], rq_rs.at[i])
        arrived(rf.at[i], rf_rs.at[i])


def home_kernel(off_ref, rkv, rq, rf, dq_ref, dk_ref, dv_ref):
    ctx = lax.axis_index("context")
    hd = lax.axis_index("heads")
    zl = lax.rem(ctx, 4)
    row = iota((256, 256), 0)
    col = iota((1, 256), 1)
    low_half = iota((256, 128), 1) < 64
    pick = iota((1, 128), 1)
    pick_row = iota((256, 128), 0)
    for pair in range(2):
        lanes = slice(128 * pair, 128 * pair + 128)
        both_q = rq[2 * pair : 2 * pair + 2].reshape(128, 256)
        back, queries = [], []
        for h in (2 * pair, 2 * pair + 1):
            perm = (row == origin(col, off_ref[hd * 4 + h], zl)).astype(F32).astype(BF)
            back_pick = jnp.logical_and(
                pick < 16, pick_row == origin(16 * zl + (pick & 15), off_ref[hd * 4 + h], zl)
            )
            far = jnp.concatenate([rf[h], jnp.zeros((112, 128), F32)], axis=0)
            high = far.astype(BF)
            low = (far - high.astype(F32)).astype(BF)
            back_pick = back_pick.astype(F32).astype(BF)
            back.append(nt(perm, rkv[h]) + nn(back_pick, high) + nn(back_pick, low))
            queries.append(nt(perm, both_q))
        dq_ref[:, lanes] = jnp.where(low_half, queries[0], queries[1]).astype(BF)
        dk_ref[:, lanes] = jnp.where(low_half, back[0], pltpu.roll(back[1], 64, 1)).astype(BF)
        dv_ref[:, lanes] = jnp.where(low_half, pltpu.roll(back[0], 64, 1), back[1]).astype(BF)


def solution(mesh):
    nseg = mesh.shape["context"] // Z
    vmem = pl.BlockSpec(memory_space=pltpu.VMEM)
    smem = pl.BlockSpec(memory_space=pltpu.SMEM)
    hbm = pl.BlockSpec(memory_space=pltpu.HBM)
    dma = pltpu.SemaphoreType.DMA

    def body(upstream, out_weight, query_rows, key_rows, value_rows, head_offsets):
        width = upstream.shape[1]
        rkv, rq, rf = pl.pallas_call(
            functools.partial(attn_kernel, nseg),
            out_shape=(
                jax.ShapeDtypeStruct((4, 128, 256), BF),
                jax.ShapeDtypeStruct((4, 64, 256), BF),
                jax.ShapeDtypeStruct((4, 16, 128), F32),
            ),
            in_specs=[hbm] * 6,
            out_specs=(hbm, hbm, hbm),
            scratch_shapes=[
                pltpu.SMEM((16,), jnp.int32),
                pltpu.VMEM(out_weight.shape, BF),
                pltpu.VMEM(query_rows.shape, BF),
                pltpu.VMEM(key_rows.shape, BF),
                pltpu.VMEM(value_rows.shape, BF),
                pltpu.VMEM((4, 256, 128), BF),
                pltpu.VMEM((4, 64, 256), BF),
                pltpu.VMEM((4, 64, 256), BF),
                pltpu.VMEM((Z, 256, 128), BF),
                pltpu.VMEM((Z, 64, 256), BF),
                pltpu.VMEM((4, 128, 256), BF),
                pltpu.VMEM((4, 128, 256), BF),
                pltpu.VMEM((4, 64, width), BF),
                pltpu.VMEM((64, 128), BF),
                pltpu.VMEM((nseg, 2, 64, 128), BF),
                pltpu.VMEM((64, nseg * 128), BF),
                pltpu.VMEM((Z, 4, 256, 256), F32),
                pltpu.VMEM((Z, 4, 256, 256), F32),
                pltpu.VMEM((4, 16, 256), F32),
                pltpu.VMEM((4, 16, 256), F32),
                pltpu.VMEM((4, 16, 256), F32),
                pltpu.VMEM((nseg * 128, 128), F32),
                pltpu.VMEM((nseg * 128, 128), F32),
                pltpu.VMEM((4, 64, 256), F32),
                pltpu.VMEM((nseg, 2, 64, 128), BF),
                pltpu.VMEM((nseg, 2, 64, 128), BF),
                pltpu.VMEM((4, 128, 256), BF),
                pltpu.VMEM((4, 128, 256), BF),
                pltpu.VMEM((4, 128, 256), BF),
                pltpu.VMEM((4, 64, 256), BF),
                pltpu.VMEM((4, 16, 128), F32),
                dma((6,)),
                dma((3,)), dma((3,)),
                dma((4,)), dma((4,)),
                dma((4,)), dma((Z,)), dma((4,)),
                dma((4,)), dma((4,)),
                dma((4,)), dma((4,)),
                dma((nseg, 2)), dma((nseg, 2)),
                dma((nseg, 2)), dma((nseg, 2)),
                dma((4,)), dma((4,)),
                dma((4,)), dma((4,)),
                dma((4,)), dma((4,)),
                dma((4,)), dma((4,)),
            ],
            compiler_params=pltpu.CompilerParams(
                collective_id=0, has_side_effects=True, vmem_limit_bytes=66400000
            ),
            name="attn",
        )(head_offsets, upstream, out_weight, query_rows, key_rows, value_rows)
        block = jax.ShapeDtypeStruct(query_rows.shape, BF)
        return pl.pallas_call(
            home_kernel,
            out_shape=(block, block, block),
            in_specs=[smem, vmem, vmem, vmem],
            out_specs=(vmem, vmem, vmem),
            name="home",
        )(head_offsets, rkv, rq, rf)

    return jax.shard_map(
        body,
        mesh=mesh,
        in_specs=(
            P(("context", "heads"), None),
            P("heads", None),
            P("context", "heads"),
            P("context", "heads"),
            P("context", "heads"),
            P(),
        ),
        out_specs=(P("context", "heads"), P("context", "heads"), P("context", "heads")),
        check_vma=False,
    )
```

```python
import functools

import jax
import jax.numpy as jnp
from jax import lax
from jax.experimental import pallas as pl
from jax.experimental.pallas import tpu as pltpu
from jax.sharding import PartitionSpec as P

Z = 8
RATE = 16
BF = jnp.bfloat16
F32 = jnp.float32
MESH = pl.DeviceIdType.MESH
LOW = -1e30


def nn(a, b):
    return lax.dot_general(a, b, (((1,), (0,)), ((), ())), preferred_element_type=F32)


def nt(a, b):
    return lax.dot_general(a, b, (((1,), (1,)), ((), ())), preferred_element_type=F32)


def iota(shape, dim):
    return lax.broadcasted_iota(jnp.int32, shape, dim)


def place(rows, offset, zl):
    return 16 * (((rows & 15) - offset + zl + 16) & 15) + (rows >> 4)


def origin(places, offset, zl):
    return 16 * (places & 15) + (((places >> 4) + offset - zl + 16) & 15)


def attn_kernel(
    nseg,
    off_h, up_h, w_h, q_h, k_h, v_h,
    rkv, rq, rf,
    off_ref, w_ref, q_ref, k_ref, v_ref,
    kvs, qts, ots, kv, kt, qt, ot, up, pick, fk, fkt, ex, dp,
    m_s, l_s, f_s, fe, fds, acc_s, fse, fre, sse, sre, rks, rqs, rfs,
    in_s, up_ss, up_rs, qt_ss, qt_rs, kv_ss, kv_rs, fw_ss, ot_ss, ot_rs, pk_ss, pk_rs,
    fa_ss, fa_rs, fb_ss, fb_rs, si_ss, si_rs, rk_ss, rk_rs, rq_ss, rq_rs, rf_ss, rf_rs,
):
    ctx = lax.axis_index("context")
    hd = lax.axis_index("heads")
    s = lax.div(ctx, Z)
    z = lax.rem(ctx, Z)
    xh = lax.div(hd, 2)
    c = lax.rem(hd, 2)
    zh = lax.div(z, 4)
    zl = lax.rem(z, 4)
    oc = 1 - c

    def dev(sv, zv, xv, cv):
        return {"context": sv * Z + zv, "heads": xv * 2 + cv}

    sibling = dev(s, z, xh, oc)
    partner = dev(s, z, 1 - xh, c)

    def peer(i):
        return dev(s, 4 * c + i, xh, zh)

    def far_seg(t):
        return lax.rem(s + t, nseg)

    def is_me(i):
        return jnp.logical_and(zh == c, zl == i)

    def rdma(src, dst, ss, rs, device):
        return pltpu.make_async_remote_copy(
            src_ref=src, dst_ref=dst, send_sem=ss, recv_sem=rs, device_id=device, device_id_type=MESH
        )

    def peer_send(src, dst, ss, rs, i):
        me = is_me(i)

        @pl.when(me)
        def _():
            pltpu.make_async_copy(src, dst, rs).start()

        @pl.when(jnp.logical_not(me))
        def _():
            rdma(src, dst, ss, rs, peer(i)).start()

    def peer_sent(src, ss, i):
        @pl.when(jnp.logical_not(is_me(i)))
        def _():
            rdma(src, src, ss, ss, peer(i)).wait_send()

    def arrived(dst, rs):
        pltpu.make_async_copy(dst, dst, rs).wait()

    code = jnp.where(zl < 2, jnp.where(zl == 0, 228, 225), jnp.where(zl == 2, 54, 27))
    near_last = [lax.rem(lax.div(code, 4**j), 4) for j in range(4)]

    def order_of(half, j):
        return jnp.where(half == zh, near_last[3 - j], near_last[j])

    def order(j):
        return order_of(c, j)

    def step_of(half, j):
        out = order_of(half, 3)
        for n in range(3):
            out = jnp.where(j == n, order_of(half, n), out)
        return out

    bar = pltpu.get_barrier_semaphore()

    def hello(device):
        pl.semaphore_signal(bar, inc=1, device_id=device, device_id_type=MESH)

    for i in range(4):
        @pl.when(jnp.logical_not(is_me(i)))
        def _():
            hello(peer(i))
    hello(sibling)
    hello(partner)
    for t in range(1, nseg):
        for cc in range(2):
            hello(dev(far_seg(t), z, xh, cc))

    loads = [
        pltpu.make_async_copy(a, b, in_s.at[n])
        for n, (a, b) in enumerate(
            ((off_h, off_ref), (q_h, q_ref), (k_h, k_ref), (v_h, v_ref), (up_h, up.at[hd]), (w_h, w_ref))
        )
    ]
    for load in loads:
        load.start()

    for b in range(4):
        qt[b, 64:128, :] = jnp.zeros((64, 256), BF)
        ot[b, 0:64, :] = jnp.zeros((64, 256), BF)
    m_s[...] = jnp.full(m_s.shape, LOW, F32)
    l_s[...] = jnp.zeros(l_s.shape, F32)
    row = iota((1, 256), 1)
    col = iota((256, 256), 0)
    low_half = iota((256, 128), 1) < 64
    lane = iota((1, 128), 1)

    for load in loads[:4]:
        load.wait()
    q_t = q_ref[...].astype(F32).T.astype(BF)
    k_v = [
        jnp.concatenate([k_ref[:, n : n + 128], v_ref[:, n : n + 128]], axis=1) for n in (0, 128)
    ]
    perms = []
    for h in range(4):
        perm = (col == place(row, off_ref[hd * 4 + h], zl)).astype(F32).astype(BF)
        perms.append(perm)
        qts[h] = (nt(q_t[64 * h : 64 * h + 64, :], perm) * 0.125).astype(BF)
        both = nn(perm, k_v[h // 2])
        k_p = both[:, 0:128]
        v_p = both[:, 128:256]
        if h % 2:
            k_p = pltpu.roll(k_p, 64, 1)
        else:
            v_p = pltpu.roll(v_p, 64, 1)
        kvs[h] = jnp.where(low_half, k_p, v_p).astype(BF)
    loads[4].wait()

    pl.semaphore_wait(bar, 4 + 2 + 2 * (nseg - 1) - jnp.where(zh == c, 1, 0))

    picked = pl.ds(pl.multiple_of(16 * zl, 16), 16)
    rdma(up.at[hd], up.at[hd], up_ss.at[0], up_rs.at[0], partner).start()
    rdma(up.at[hd], up.at[hd], up_ss.at[1], up_rs.at[1], sibling).start()
    for j in range(4):
        i = order(j)
        peer_send(kvs.at[i, picked, :], pick.at[picked, :], pk_ss.at[i], pk_rs.at[zl], i)
    for j in range(4):
        i = order(j)
        peer_send(qts.at[i], qt.at[zl, 0:64, :], qt_ss.at[i], qt_rs.at[zl], i)
    for j in range(4):
        i = order(j)
        peer_send(kvs.at[i], kv.at[z], kv_ss.at[i], kv_rs.at[z], i)

    for i in range(4):
        arrived(pick.at[16 * i : 16 * i + 16, :], pk_rs.at[i])
    for t in range(1, nseg):
        for cc in range(2):
            rdma(
                pick, fk.at[s, c], fa_ss.at[t, cc], fa_rs.at[s, c], dev(far_seg(t), z, xh, cc)
            ).start()
    rdma(pick, fk.at[s, c], fa_ss.at[0, 0], fa_rs.at[s, c], sibling).start()
    fk[s, c] = pick[...]

    far_hd = (1 - xh) * 2 + c
    arrived(up.at[far_hd], up_rs.at[0])
    rdma(up.at[far_hd], up.at[far_hd], up_ss.at[2], up_rs.at[2], sibling).start()
    arrived(up.at[xh * 2 + oc], up_rs.at[1])
    loads[5].wait()
    arrived(up.at[(1 - xh) * 2 + oc], up_rs.at[2])
    a_t = nt(w_ref[...], up[...].reshape(256, up.shape[2])).astype(BF)
    for h in range(4):
        ots[h] = nt(a_t[64 * h : 64 * h + 64, :], perms[h]).astype(BF)
    for j in range(4):
        i = order(j)
        peer_send(ots.at[i], ot.at[zl, 64:128, :], ot_ss.at[i], ot_rs.at[zl], i)

    for i in range(4):
        arrived(qt.at[i, 0:64, :], qt_rs.at[i])

    def score_block(d):
        keys = kv[d]
        kt[d] = keys.astype(F32).T[0:64, :].astype(BF)
        for b in range(4):
            st = nn(keys, qt[b])
            mb = jnp.max(st, axis=0, keepdims=True)
            e = jnp.exp(st - mb)
            ex[d, b] = e
            m_s[b, pl.ds(d, 1), :] = mb
            l_s[b, pl.ds(d, 1), :] = jnp.sum(e, axis=0, keepdims=True)

    def own_block(j, carry):
        i = step_of(c, j)
        d = 4 * c + i
        arrived(kv.at[d], kv_rs.at[d])
        rdma(kv.at[d], kv.at[d], fw_ss.at[i], kv_rs.at[d], sibling).start()
        score_block(d)
        return carry

    def other_block(j, carry):
        d = 4 * oc + step_of(oc, j)
        arrived(kv.at[d], kv_rs.at[d])
        score_block(d)
        return carry

    lax.fori_loop(0, 4, own_block, 0)
    lax.fori_loop(0, 4, other_block, 0)

    def mine(b):
        return jnp.logical_and(lane >= 16 * b, lane < 16 * b + 16)

    def gather_lanes(parts):
        out = jnp.zeros(parts[0].shape, parts[0].dtype)
        for b in range(4):
            out = jnp.where(mine(b), parts[b], out)
        return out

    q_far = gather_lanes([qt[b, :, 0:128].astype(F32) for b in range(4)]).astype(BF)
    for t in range(1, nseg):
        for cc in range(2):
            arrived(fk.at[far_seg(t), cc], fa_rs.at[far_seg(t), cc])
    arrived(fk.at[s, oc], fa_rs.at[s, oc])
    far_keys = fk[...].reshape(nseg * 128, 128)
    fkt[...] = far_keys.astype(F32).T[0:64, :].astype(BF)
    st = nn(far_keys, q_far)
    m_far = jnp.max(st, axis=0, keepdims=True)
    e_far = jnp.exp(st - m_far)
    fe[...] = e_far
    l_far = jnp.sum(e_far, axis=0, keepdims=True)
    for b in range(4):
        m_s[b, Z : Z + 1, 0:128] = jnp.where(mine(b), m_far, LOW)
        l_s[b, Z : Z + 1, 0:128] = jnp.where(mine(b), l_far, 0.0)
    for b in range(4):
        m_all = m_s[b]
        m_row = jnp.max(m_all, axis=0, keepdims=True)
        lse = m_row + jnp.log(jnp.sum(l_s[b] * jnp.exp(m_all - m_row), axis=0, keepdims=True))
        f_s[b] = jnp.exp(m_all - lse)
    fe[...] = fe[...] * gather_lanes([f_s[b, Z : Z + 1, 0:128] for b in range(4)])

    for j in range(4):
        b = order(j)
        arrived(ot.at[b, 64:128, :], ot_rs.at[b])
        o_b = ot[b]

        def dprob_blocks(n, total):
            for m in range(4):
                d = 4 * n + m
                g = nn(kv[d], o_b)
                dp[d, b] = g
                part = jnp.sum(ex[d, b] * g, axis=0, keepdims=True)
                total = total + f_s[b, pl.ds(d, 1), :] * part
            return total

        l_s[b, 0:1, :] = lax.fori_loop(0, 2, dprob_blocks, jnp.zeros((1, 256), F32))

    o_far = gather_lanes([ot[b, :, 0:128].astype(F32) for b in range(4)]).astype(BF)
    g_far = nn(fk[...].reshape(nseg * 128, 128), o_far)
    fds[...] = g_far
    far_delta = jnp.sum(fe[...] * g_far, axis=0, keepdims=True)
    zero_row = jnp.zeros((1, 128), F32)
    delta = [
        l_s[b, 0:1, :] + jnp.concatenate([jnp.where(mine(b), far_delta, 0.0), zero_row], axis=1)
        for b in range(4)
    ]
    for b in range(4):
        l_s[b, 0:1, :] = delta[b]

    for b in range(4):
        acc_s[b] = jnp.zeros((64, 256), F32)

    def grad_block(d):
        key_grads = jnp.zeros((64, 256), F32)
        value_grads = jnp.zeros((64, 256), F32)
        keys_t = kt[d]
        for b in range(4):
            p = ex[d, b] * f_s[b, pl.ds(d, 1), :]
            ds = (p * (dp[d, b] - l_s[b, 0:1, :])).astype(BF)
            key_grads = key_grads + nt(qt[b, 0:64, :], ds)
            value_grads = value_grads + nt(ot[b, 64:128, :], p.astype(BF))
            acc_s[b] = acc_s[b] + nn(keys_t, ds)
        return jnp.concatenate([key_grads, value_grads], axis=0)

    def pair_block(n, carry):
        i = step_of(oc, n)
        sse[i] = grad_block(4 * oc + i).astype(BF)
        rdma(sse.at[i], sre.at[i], si_ss.at[i], si_rs.at[i], sibling).start()
        i = step_of(c, n)
        grads = grad_block(4 * c + i)
        arrived(sre.at[i], si_rs.at[i])
        rks[i] = (grads + sre[i].astype(F32)).astype(BF)
        peer_send(rks.at[i], rkv.at[zl], rk_ss.at[i], rk_rs.at[zl], i)
        return carry

    lax.fori_loop(0, 1, pair_block, 0)

    p_far = fe[...]
    ds_far = (p_far * (fds[...] - gather_lanes([delta[b][:, 0:128] for b in range(4)]))).astype(BF)
    dkv_far = nt(ds_far, q_far) + nt(p_far.astype(BF), o_far)
    fse[...] = dkv_far.astype(BF).reshape(nseg, 2, 64, 128)
    for t in range(1, nseg):
        for cc in range(2):
            rdma(
                fse.at[far_seg(t), cc], fre.at[s, c], fb_ss.at[t, cc], fb_rs.at[s, c],
                dev(far_seg(t), z, xh, cc),
            ).start()
    rdma(fse.at[s, oc], fre.at[s, c], fb_ss.at[0, 0], fb_rs.at[s, c], sibling).start()
    fre[s, c] = fse[s, c]
    dq_far = nn(fkt[...], ds_far)
    for b in range(4):
        acc_s[b, :, 0:128] = acc_s[b, :, 0:128] + jnp.where(mine(b), dq_far, 0.0)

    lax.fori_loop(1, 4, pair_block, 0)
    for j in range(4):
        b = order(j)
        rqs[b] = (acc_s[b] * 0.125).astype(BF)
        peer_send(rqs.at[b], rq.at[zl], rq_ss.at[b], rq_rs.at[zl], b)

    for t in range(1, nseg):
        for cc in range(2):
            arrived(fre.at[far_seg(t), cc], fb_rs.at[far_seg(t), cc])
    arrived(fre.at[s, oc], fb_rs.at[s, oc])
    fsum = jnp.zeros((64, 128), F32)
    for t in range(nseg):
        for cc in range(2):
            fsum = fsum + fre[t, cc].astype(F32)
    for i in range(4):
        rfs[i] = fsum[16 * i : 16 * i + 16, :]
    for j in range(4):
        i = order(j)
        peer_send(rfs.at[i], rf.at[zl], rf_ss.at[i], rf_rs.at[zl], i)

    for n, device in ((0, partner), (1, sibling), (2, sibling)):
        rdma(up.at[0], up.at[0], up_ss.at[n], up_ss.at[n], device).wait_send()
    for i in range(4):
        peer_sent(kvs.at[i, 0:16, :], pk_ss.at[i], i)
        peer_sent(qts.at[i], qt_ss.at[i], i)
        peer_sent(kvs.at[i], kv_ss.at[i], i)
        peer_sent(ots.at[i], ot_ss.at[i], i)
        peer_sent(rks.at[i], rk_ss.at[i], i)
        peer_sent(rqs.at[i], rq_ss.at[i], i)
        peer_sent(rfs.at[i], rf_ss.at[i], i)
        rdma(kvs.at[i], kvs.at[i], fw_ss.at[i], fw_ss.at[i], sibling).wait_send()
        rdma(sse.at[i], sse.at[i], si_ss.at[i], si_ss.at[i], sibling).wait_send()
    for t in range(1, nseg):
        for cc in range(2):
            device = dev(far_seg(t), z, xh, cc)
            rdma(pick, pick, fa_ss.at[t, cc], fa_ss.at[t, cc], device).wait_send()
            rdma(pick, pick, fb_ss.at[t, cc], fb_ss.at[t, cc], device).wait_send()
    rdma(pick, pick, fa_ss.at[0, 0], fa_ss.at[0, 0], sibling).wait_send()
    rdma(pick, pick, fb_ss.at[0, 0], fb_ss.at[0, 0], sibling).wait_send()

    for i in range(4):
        arrived(rkv.at[i], rk_rs.at[i])
        arrived(rq.at[i], rq_rs.at[i])
        arrived(rf.at[i], rf_rs.at[i])


def home_kernel(off_ref, rkv, rq, rf, dq_ref, dk_ref, dv_ref):
    ctx = lax.axis_index("context")
    hd = lax.axis_index("heads")
    zl = lax.rem(ctx, 4)
    row = iota((256, 256), 0)
    col = iota((1, 256), 1)
    low_half = iota((256, 128), 1) < 64
    pick = iota((1, 128), 1)
    pick_row = iota((256, 128), 0)
    for pair in range(2):
        lanes = slice(128 * pair, 128 * pair + 128)
        both_q = rq[2 * pair : 2 * pair + 2].reshape(128, 256)
        back, queries = [], []
        for h in (2 * pair, 2 * pair + 1):
            perm = (row == origin(col, off_ref[hd * 4 + h], zl)).astype(F32).astype(BF)
            back_pick = jnp.logical_and(
                pick < 16, pick_row == origin(16 * zl + (pick & 15), off_ref[hd * 4 + h], zl)
            )
            far = jnp.concatenate([rf[h], jnp.zeros((112, 128), F32)], axis=0)
            high = far.astype(BF)
            low = (far - high.astype(F32)).astype(BF)
            back_pick = back_pick.astype(F32).astype(BF)
            back.append(nt(perm, rkv[h]) + nn(back_pick, high) + nn(back_pick, low))
            queries.append(nt(perm, both_q))
        dq_ref[:, lanes] = jnp.where(low_half, queries[0], queries[1]).astype(BF)
        dk_ref[:, lanes] = jnp.where(low_half, back[0], pltpu.roll(back[1], 64, 1)).astype(BF)
        dv_ref[:, lanes] = jnp.where(low_half, pltpu.roll(back[0], 64, 1), back[1]).astype(BF)


def solution(mesh):
    nseg = mesh.shape["context"] // Z
    vmem = pl.BlockSpec(memory_space=pltpu.VMEM)
    smem = pl.BlockSpec(memory_space=pltpu.SMEM)
    hbm = pl.BlockSpec(memory_space=pltpu.HBM)
    dma = pltpu.SemaphoreType.DMA

    def body(upstream, out_weight, query_rows, key_rows, value_rows, head_offsets):
        width = upstream.shape[1]
        rkv, rq, rf = pl.pallas_call(
            functools.partial(attn_kernel, nseg),
            out_shape=(
                jax.ShapeDtypeStruct((4, 128, 256), BF),
                jax.ShapeDtypeStruct((4, 64, 256), BF),
                jax.ShapeDtypeStruct((4, 16, 128), F32),
            ),
            in_specs=[hbm] * 6,
            out_specs=(hbm, hbm, hbm),
            scratch_shapes=[
                pltpu.SMEM((16,), jnp.int32),
                pltpu.VMEM(out_weight.shape, BF),
                pltpu.VMEM(query_rows.shape, BF),
                pltpu.VMEM(key_rows.shape, BF),
                pltpu.VMEM(value_rows.shape, BF),
                pltpu.VMEM((4, 256, 128), BF),
                pltpu.VMEM((4, 64, 256), BF),
                pltpu.VMEM((4, 64, 256), BF),
                pltpu.VMEM((Z, 256, 128), BF),
                pltpu.VMEM((Z, 64, 256), BF),
                pltpu.VMEM((4, 128, 256), BF),
                pltpu.VMEM((4, 128, 256), BF),
                pltpu.VMEM((4, 64, width), BF),
                pltpu.VMEM((64, 128), BF),
                pltpu.VMEM((nseg, 2, 64, 128), BF),
                pltpu.VMEM((64, nseg * 128), BF),
                pltpu.VMEM((Z, 4, 256, 256), F32),
                pltpu.VMEM((Z, 4, 256, 256), F32),
                pltpu.VMEM((4, 16, 256), F32),
                pltpu.VMEM((4, 16, 256), F32),
                pltpu.VMEM((4, 16, 256), F32),
                pltpu.VMEM((nseg * 128, 128), F32),
                pltpu.VMEM((nseg * 128, 128), F32),
                pltpu.VMEM((4, 64, 256), F32),
                pltpu.VMEM((nseg, 2, 64, 128), BF),
                pltpu.VMEM((nseg, 2, 64, 128), BF),
                pltpu.VMEM((4, 128, 256), BF),
                pltpu.VMEM((4, 128, 256), BF),
                pltpu.VMEM((4, 128, 256), BF),
                pltpu.VMEM((4, 64, 256), BF),
                pltpu.VMEM((4, 16, 128), F32),
                dma((6,)),
                dma((3,)), dma((3,)),
                dma((4,)), dma((4,)),
                dma((4,)), dma((Z,)), dma((4,)),
                dma((4,)), dma((4,)),
                dma((4,)), dma((4,)),
                dma((nseg, 2)), dma((nseg, 2)),
                dma((nseg, 2)), dma((nseg, 2)),
                dma((4,)), dma((4,)),
                dma((4,)), dma((4,)),
                dma((4,)), dma((4,)),
                dma((4,)), dma((4,)),
            ],
            compiler_params=pltpu.CompilerParams(
                collective_id=0, has_side_effects=True, vmem_limit_bytes=66400000
            ),
            name="attn",
        )(head_offsets, upstream, out_weight, query_rows, key_rows, value_rows)
        block = jax.ShapeDtypeStruct(query_rows.shape, BF)
        return pl.pallas_call(
            home_kernel,
            out_shape=(block, block, block),
            in_specs=[smem, vmem, vmem, vmem],
            out_specs=(vmem, vmem, vmem),
            name="home",
        )(head_offsets, rkv, rq, rf)

    return jax.shard_map(
        body,
        mesh=mesh,
        in_specs=(
            P(("context", "heads"), None),
            P("heads", None),
            P("context", "heads"),
            P("context", "heads"),
            P("context", "heads"),
            P(),
        ),
        out_specs=(P("context", "heads"), P("context", "heads"), P("context", "heads")),
        check_vma=False,
    )
```

```python
import functools

import jax
import jax.numpy as jnp
from jax import lax
from jax.experimental import pallas as pl
from jax.experimental.pallas import tpu as pltpu
from jax.sharding import PartitionSpec as P

Z = 8
RATE = 16
BF = jnp.bfloat16
F32 = jnp.float32
MESH = pl.DeviceIdType.MESH
LOW = -1e30


def nn(a, b):
    return lax.dot_general(a, b, (((1,), (0,)), ((), ())), preferred_element_type=F32)


def nt(a, b):
    return lax.dot_general(a, b, (((1,), (1,)), ((), ())), preferred_element_type=F32)


def iota(shape, dim):
    return lax.broadcasted_iota(jnp.int32, shape, dim)


def place(rows, offset, zl):
    return 16 * (((rows & 15) - offset + zl + 16) & 15) + (rows >> 4)


def origin(places, offset, zl):
    return 16 * (places & 15) + (((places >> 4) + offset - zl + 16) & 15)


def attn_kernel(
    nseg,
    off_h, up_h, w_h, q_h, k_h, v_h,
    rkv, rq, rf,
    off_ref, w_ref, q_ref, k_ref, v_ref,
    kvs, qts, ots, kv, kt, qt, ot, up, pick, fk, fkt, ex, dp,
    m_s, l_s, f_s, fe, fds, acc_s, fse, fre, sse, sre, rks, rqs, rfs,
    in_s, up_ss, up_rs, qt_ss, qt_rs, kv_ss, kv_rs, fw_ss, ot_ss, ot_rs, pk_ss, pk_rs,
    fa_ss, fa_rs, fb_ss, fb_rs, si_ss, si_rs, rk_ss, rk_rs, rq_ss, rq_rs, rf_ss, rf_rs,
):
    ctx = lax.axis_index("context")
    hd = lax.axis_index("heads")
    s = lax.div(ctx, Z)
    z = lax.rem(ctx, Z)
    xh = lax.div(hd, 2)
    c = lax.rem(hd, 2)
    zh = lax.div(z, 4)
    zl = lax.rem(z, 4)
    oc = 1 - c

    def dev(sv, zv, xv, cv):
        return {"context": sv * Z + zv, "heads": xv * 2 + cv}

    sibling = dev(s, z, xh, oc)
    partner = dev(s, z, 1 - xh, c)

    def peer(i):
        return dev(s, 4 * c + i, xh, zh)

    def far_seg(t):
        return lax.rem(s + t, nseg)

    def is_me(i):
        return jnp.logical_and(zh == c, zl == i)

    def rdma(src, dst, ss, rs, device):
        return pltpu.make_async_remote_copy(
            src_ref=src, dst_ref=dst, send_sem=ss, recv_sem=rs, device_id=device, device_id_type=MESH
        )

    def peer_send(src, dst, ss, rs, i):
        me = is_me(i)

        @pl.when(me)
        def _():
            pltpu.make_async_copy(src, dst, rs).start()

        @pl.when(jnp.logical_not(me))
        def _():
            rdma(src, dst, ss, rs, peer(i)).start()

    def peer_sent(src, ss, i):
        @pl.when(jnp.logical_not(is_me(i)))
        def _():
            rdma(src, src, ss, ss, peer(i)).wait_send()

    def arrived(dst, rs):
        pltpu.make_async_copy(dst, dst, rs).wait()

    code = jnp.where(zl < 2, jnp.where(zl == 0, 228, 225), jnp.where(zl == 2, 54, 27))
    near_last = [lax.rem(lax.div(code, 4**j), 4) for j in range(4)]

    def order_of(half, j):
        return jnp.where(half == zh, near_last[3 - j], near_last[j])

    def order(j):
        return order_of(c, j)

    def step_of(half, j):
        out = order_of(half, 3)
        for n in range(3):
            out = jnp.where(j == n, order_of(half, n), out)
        return out

    bar = pltpu.get_barrier_semaphore()

    def hello(device):
        pl.semaphore_signal(bar, inc=1, device_id=device, device_id_type=MESH)

    for i in range(4):
        @pl.when(jnp.logical_not(is_me(i)))
        def _():
            hello(peer(i))
    hello(sibling)
    hello(partner)
    for t in range(1, nseg):
        for cc in range(2):
            hello(dev(far_seg(t), z, xh, cc))

    loads = [
        pltpu.make_async_copy(a, b, in_s.at[n])
        for n, (a, b) in enumerate(
            ((off_h, off_ref), (q_h, q_ref), (k_h, k_ref), (v_h, v_ref), (up_h, up.at[hd]), (w_h, w_ref))
        )
    ]
    for load in loads:
        load.start()

    for b in range(4):
        qt[b, 64:128, :] = jnp.zeros((64, 256), BF)
        ot[b, 0:64, :] = jnp.zeros((64, 256), BF)
    m_s[...] = jnp.full(m_s.shape, LOW, F32)
    l_s[...] = jnp.zeros(l_s.shape, F32)
    row = iota((1, 256), 1)
    col = iota((256, 256), 0)
    low_half = iota((256, 128), 1) < 64
    lane = iota((1, 128), 1)

    for load in loads[:2]:
        load.wait()
    q_t = q_ref[...].astype(F32).T.astype(BF)
    perms = []
    for h in range(4):
        perm = (col == place(row, off_ref[hd * 4 + h], zl)).astype(F32).astype(BF)
        perms.append(perm)
        qts[h] = (nt(q_t[64 * h : 64 * h + 64, :], perm) * 0.125).astype(BF)
    loads[4].wait()

    pl.semaphore_wait(bar, 4 + 2 + 2 * (nseg - 1) - jnp.where(zh == c, 1, 0))

    rdma(up.at[hd], up.at[hd], up_ss.at[0], up_rs.at[0], partner).start()
    rdma(up.at[hd], up.at[hd], up_ss.at[1], up_rs.at[1], sibling).start()
    for j in range(4):
        i = order(j)
        peer_send(qts.at[i], qt.at[zl, 0:64, :], qt_ss.at[i], qt_rs.at[zl], i)

    for load in loads[2:4]:
        load.wait()
    k_v = [
        jnp.concatenate([k_ref[:, n : n + 128], v_ref[:, n : n + 128]], axis=1) for n in (0, 128)
    ]
    for h in range(4):
        both = nn(perms[h], k_v[h // 2])
        k_p = both[:, 0:128]
        v_p = both[:, 128:256]
        if h % 2:
            k_p = pltpu.roll(k_p, 64, 1)
        else:
            v_p = pltpu.roll(v_p, 64, 1)
        kvs[h] = jnp.where(low_half, k_p, v_p).astype(BF)
    picked = pl.ds(pl.multiple_of(16 * zl, 16), 16)
    for j in range(4):
        i = order(j)
        peer_send(kvs.at[i, picked, :], pick.at[picked, :], pk_ss.at[i], pk_rs.at[zl], i)
    for j in range(4):
        i = order(j)
        peer_send(kvs.at[i], kv.at[z], kv_ss.at[i], kv_rs.at[z], i)

    for i in range(4):
        arrived(pick.at[16 * i : 16 * i + 16, :], pk_rs.at[i])
    for t in range(1, nseg):
        for cc in range(2):
            rdma(
                pick, fk.at[s, c], fa_ss.at[t, cc], fa_rs.at[s, c], dev(far_seg(t), z, xh, cc)
            ).start()
    rdma(pick, fk.at[s, c], fa_ss.at[0, 0], fa_rs.at[s, c], sibling).start()
    fk[s, c] = pick[...]

    far_hd = (1 - xh) * 2 + c
    arrived(up.at[far_hd], up_rs.at[0])
    rdma(up.at[far_hd], up.at[far_hd], up_ss.at[2], up_rs.at[2], sibling).start()
    arrived(up.at[xh * 2 + oc], up_rs.at[1])
    loads[5].wait()
    arrived(up.at[(1 - xh) * 2 + oc], up_rs.at[2])
    a_t = nt(w_ref[...], up[...].reshape(256, up.shape[2])).astype(BF)
    for h in range(4):
        ots[h] = nt(a_t[64 * h : 64 * h + 64, :], perms[h]).astype(BF)
    for j in range(4):
        i = order(j)
        peer_send(ots.at[i], ot.at[zl, 64:128, :], ot_ss.at[i], ot_rs.at[zl], i)

    for i in range(4):
        arrived(qt.at[i, 0:64, :], qt_rs.at[i])

    def score_block(d):
        keys = kv[d]
        kt[d] = keys.astype(F32).T[0:64, :].astype(BF)
        for b in range(4):
            st = nn(keys, qt[b])
            mb = jnp.max(st, axis=0, keepdims=True)
            e = jnp.exp(st - mb)
            ex[d, b] = e
            m_s[b, pl.ds(d, 1), :] = mb
            l_s[b, pl.ds(d, 1), :] = jnp.sum(e, axis=0, keepdims=True)

    def own_block(j, carry):
        i = step_of(c, j)
        d = 4 * c + i
        arrived(kv.at[d], kv_rs.at[d])
        rdma(kv.at[d], kv.at[d], fw_ss.at[i], kv_rs.at[d], sibling).start()
        score_block(d)
        return carry

    def other_block(j, carry):
        d = 4 * oc + step_of(oc, j)
        arrived(kv.at[d], kv_rs.at[d])
        score_block(d)
        return carry

    lax.fori_loop(0, 4, own_block, 0)
    lax.fori_loop(0, 4, other_block, 0)

    def mine(b):
        return jnp.logical_and(lane >= 16 * b, lane < 16 * b + 16)

    def gather_lanes(parts):
        out = jnp.zeros(parts[0].shape, parts[0].dtype)
        for b in range(4):
            out = jnp.where(mine(b), parts[b], out)
        return out

    q_far = gather_lanes([qt[b, :, 0:128].astype(F32) for b in range(4)]).astype(BF)
    for t in range(1, nseg):
        for cc in range(2):
            arrived(fk.at[far_seg(t), cc], fa_rs.at[far_seg(t), cc])
    arrived(fk.at[s, oc], fa_rs.at[s, oc])
    far_keys = fk[...].reshape(nseg * 128, 128)
    fkt[...] = far_keys.astype(F32).T[0:64, :].astype(BF)
    st = nn(far_keys, q_far)
    m_far = jnp.max(st, axis=0, keepdims=True)
    e_far = jnp.exp(st - m_far)
    fe[...] = e_far
    l_far = jnp.sum(e_far, axis=0, keepdims=True)
    for b in range(4):
        m_s[b, Z : Z + 1, 0:128] = jnp.where(mine(b), m_far, LOW)
        l_s[b, Z : Z + 1, 0:128] = jnp.where(mine(b), l_far, 0.0)
    for b in range(4):
        m_all = m_s[b]
        m_row = jnp.max(m_all, axis=0, keepdims=True)
        lse = m_row + jnp.log(jnp.sum(l_s[b] * jnp.exp(m_all - m_row), axis=0, keepdims=True))
        f_s[b] = jnp.exp(m_all - lse)
    fe[...] = fe[...] * gather_lanes([f_s[b, Z : Z + 1, 0:128] for b in range(4)])

    for j in range(4):
        b = order(j)
        arrived(ot.at[b, 64:128, :], ot_rs.at[b])
        o_b = ot[b]

        def dprob_blocks(n, total):
            for m in range(4):
                d = 4 * n + m
                g = nn(kv[d], o_b)
                dp[d, b] = g
                part = jnp.sum(ex[d, b] * g, axis=0, keepdims=True)
                total = total + f_s[b, pl.ds(d, 1), :] * part
            return total

        l_s[b, 0:1, :] = lax.fori_loop(0, 2, dprob_blocks, jnp.zeros((1, 256), F32))

    o_far = gather_lanes([ot[b, :, 0:128].astype(F32) for b in range(4)]).astype(BF)
    g_far = nn(fk[...].reshape(nseg * 128, 128), o_far)
    fds[...] = g_far
    far_delta = jnp.sum(fe[...] * g_far, axis=0, keepdims=True)
    zero_row = jnp.zeros((1, 128), F32)
    delta = [
        l_s[b, 0:1, :] + jnp.concatenate([jnp.where(mine(b), far_delta, 0.0), zero_row], axis=1)
        for b in range(4)
    ]
    for b in range(4):
        l_s[b, 0:1, :] = delta[b]

    for b in range(4):
        acc_s[b] = jnp.zeros((64, 256), F32)

    def grad_block(d):
        key_grads = jnp.zeros((64, 256), F32)
        value_grads = jnp.zeros((64, 256), F32)
        keys_t = kt[d]
        for b in range(4):
            p = ex[d, b] * f_s[b, pl.ds(d, 1), :]
            ds = (p * (dp[d, b] - l_s[b, 0:1, :])).astype(BF)
            key_grads = key_grads + nt(qt[b, 0:64, :], ds)
            value_grads = value_grads + nt(ot[b, 64:128, :], p.astype(BF))
            acc_s[b] = acc_s[b] + nn(keys_t, ds)
        return jnp.concatenate([key_grads, value_grads], axis=0)

    def pair_block(n, carry):
        i = step_of(oc, n)
        sse[i] = grad_block(4 * oc + i).astype(BF)
        rdma(sse.at[i], sre.at[i], si_ss.at[i], si_rs.at[i], sibling).start()
        i = step_of(c, n)
        grads = grad_block(4 * c + i)
        arrived(sre.at[i], si_rs.at[i])
        rks[i] = (grads + sre[i].astype(F32)).astype(BF)
        peer_send(rks.at[i], rkv.at[zl], rk_ss.at[i], rk_rs.at[zl], i)
        return carry

    lax.fori_loop(0, 1, pair_block, 0)

    p_far = fe[...]
    ds_far = (p_far * (fds[...] - gather_lanes([delta[b][:, 0:128] for b in range(4)]))).astype(BF)
    dkv_far = nt(ds_far, q_far) + nt(p_far.astype(BF), o_far)
    fse[...] = dkv_far.astype(BF).reshape(nseg, 2, 64, 128)
    for t in range(1, nseg):
        for cc in range(2):
            rdma(
                fse.at[far_seg(t), cc], fre.at[s, c], fb_ss.at[t, cc], fb_rs.at[s, c],
                dev(far_seg(t), z, xh, cc),
            ).start()
    rdma(fse.at[s, oc], fre.at[s, c], fb_ss.at[0, 0], fb_rs.at[s, c], sibling).start()
    fre[s, c] = fse[s, c]
    dq_far = nn(fkt[...], ds_far)
    for b in range(4):
        acc_s[b, :, 0:128] = acc_s[b, :, 0:128] + jnp.where(mine(b), dq_far, 0.0)

    lax.fori_loop(1, 4, pair_block, 0)
    for j in range(4):
        b = order(j)
        rqs[b] = (acc_s[b] * 0.125).astype(BF)
        peer_send(rqs.at[b], rq.at[zl], rq_ss.at[b], rq_rs.at[zl], b)

    for t in range(1, nseg):
        for cc in range(2):
            arrived(fre.at[far_seg(t), cc], fb_rs.at[far_seg(t), cc])
    arrived(fre.at[s, oc], fb_rs.at[s, oc])
    fsum = jnp.zeros((64, 128), F32)
    for t in range(nseg):
        for cc in range(2):
            fsum = fsum + fre[t, cc].astype(F32)
    for i in range(4):
        rfs[i] = fsum[16 * i : 16 * i + 16, :]
    for j in range(4):
        i = order(j)
        peer_send(rfs.at[i], rf.at[zl], rf_ss.at[i], rf_rs.at[zl], i)

    for n, device in ((0, partner), (1, sibling), (2, sibling)):
        rdma(up.at[0], up.at[0], up_ss.at[n], up_ss.at[n], device).wait_send()
    for i in range(4):
        peer_sent(kvs.at[i, 0:16, :], pk_ss.at[i], i)
        peer_sent(qts.at[i], qt_ss.at[i], i)
        peer_sent(kvs.at[i], kv_ss.at[i], i)
        peer_sent(ots.at[i], ot_ss.at[i], i)
        peer_sent(rks.at[i], rk_ss.at[i], i)
        peer_sent(rqs.at[i], rq_ss.at[i], i)
        peer_sent(rfs.at[i], rf_ss.at[i], i)
        rdma(kvs.at[i], kvs.at[i], fw_ss.at[i], fw_ss.at[i], sibling).wait_send()
        rdma(sse.at[i], sse.at[i], si_ss.at[i], si_ss.at[i], sibling).wait_send()
    for t in range(1, nseg):
        for cc in range(2):
            device = dev(far_seg(t), z, xh, cc)
            rdma(pick, pick, fa_ss.at[t, cc], fa_ss.at[t, cc], device).wait_send()
            rdma(pick, pick, fb_ss.at[t, cc], fb_ss.at[t, cc], device).wait_send()
    rdma(pick, pick, fa_ss.at[0, 0], fa_ss.at[0, 0], sibling).wait_send()
    rdma(pick, pick, fb_ss.at[0, 0], fb_ss.at[0, 0], sibling).wait_send()

    for i in range(4):
        arrived(rkv.at[i], rk_rs.at[i])
        arrived(rq.at[i], rq_rs.at[i])
        arrived(rf.at[i], rf_rs.at[i])


def home_kernel(off_ref, rkv, rq, rf, dq_ref, dk_ref, dv_ref):
    ctx = lax.axis_index("context")
    hd = lax.axis_index("heads")
    zl = lax.rem(ctx, 4)
    row = iota((256, 256), 0)
    col = iota((1, 256), 1)
    low_half = iota((256, 128), 1) < 64
    pick = iota((1, 128), 1)
    pick_row = iota((256, 128), 0)
    for pair in range(2):
        lanes = slice(128 * pair, 128 * pair + 128)
        both_q = rq[2 * pair : 2 * pair + 2].reshape(128, 256)
        back, queries = [], []
        for h in (2 * pair, 2 * pair + 1):
            perm = (row == origin(col, off_ref[hd * 4 + h], zl)).astype(F32).astype(BF)
            back_pick = jnp.logical_and(
                pick < 16, pick_row == origin(16 * zl + (pick & 15), off_ref[hd * 4 + h], zl)
            )
            far = jnp.concatenate([rf[h], jnp.zeros((112, 128), F32)], axis=0)
            high = far.astype(BF)
            low = (far - high.astype(F32)).astype(BF)
            back_pick = back_pick.astype(F32).astype(BF)
            back.append(nt(perm, rkv[h]) + nn(back_pick, high) + nn(back_pick, low))
            queries.append(nt(perm, both_q))
        dq_ref[:, lanes] = jnp.where(low_half, queries[0], queries[1]).astype(BF)
        dk_ref[:, lanes] = jnp.where(low_half, back[0], pltpu.roll(back[1], 64, 1)).astype(BF)
        dv_ref[:, lanes] = jnp.where(low_half, pltpu.roll(back[0], 64, 1), back[1]).astype(BF)


def solution(mesh):
    nseg = mesh.shape["context"] // Z
    vmem = pl.BlockSpec(memory_space=pltpu.VMEM)
    smem = pl.BlockSpec(memory_space=pltpu.SMEM)
    hbm = pl.BlockSpec(memory_space=pltpu.HBM)
    dma = pltpu.SemaphoreType.DMA

    def body(upstream, out_weight, query_rows, key_rows, value_rows, head_offsets):
        width = upstream.shape[1]
        rkv, rq, rf = pl.pallas_call(
            functools.partial(attn_kernel, nseg),
            out_shape=(
                jax.ShapeDtypeStruct((4, 128, 256), BF),
                jax.ShapeDtypeStruct((4, 64, 256), BF),
                jax.ShapeDtypeStruct((4, 16, 128), F32),
            ),
            in_specs=[hbm] * 6,
            out_specs=(hbm, hbm, hbm),
            scratch_shapes=[
                pltpu.SMEM((16,), jnp.int32),
                pltpu.VMEM(out_weight.shape, BF),
                pltpu.VMEM(query_rows.shape, BF),
                pltpu.VMEM(key_rows.shape, BF),
                pltpu.VMEM(value_rows.shape, BF),
                pltpu.VMEM((4, 256, 128), BF),
                pltpu.VMEM((4, 64, 256), BF),
                pltpu.VMEM((4, 64, 256), BF),
                pltpu.VMEM((Z, 256, 128), BF),
                pltpu.VMEM((Z, 64, 256), BF),
                pltpu.VMEM((4, 128, 256), BF),
                pltpu.VMEM((4, 128, 256), BF),
                pltpu.VMEM((4, 64, width), BF),
                pltpu.VMEM((64, 128), BF),
                pltpu.VMEM((nseg, 2, 64, 128), BF),
                pltpu.VMEM((64, nseg * 128), BF),
                pltpu.VMEM((Z, 4, 256, 256), F32),
                pltpu.VMEM((Z, 4, 256, 256), F32),
                pltpu.VMEM((4, 16, 256), F32),
                pltpu.VMEM((4, 16, 256), F32),
                pltpu.VMEM((4, 16, 256), F32),
                pltpu.VMEM((nseg * 128, 128), F32),
                pltpu.VMEM((nseg * 128, 128), F32),
                pltpu.VMEM((4, 64, 256), F32),
                pltpu.VMEM((nseg, 2, 64, 128), BF),
                pltpu.VMEM((nseg, 2, 64, 128), BF),
                pltpu.VMEM((4, 128, 256), BF),
                pltpu.VMEM((4, 128, 256), BF),
                pltpu.VMEM((4, 128, 256), BF),
                pltpu.VMEM((4, 64, 256), BF),
                pltpu.VMEM((4, 16, 128), F32),
                dma((6,)),
                dma((3,)), dma((3,)),
                dma((4,)), dma((4,)),
                dma((4,)), dma((Z,)), dma((4,)),
                dma((4,)), dma((4,)),
                dma((4,)), dma((4,)),
                dma((nseg, 2)), dma((nseg, 2)),
                dma((nseg, 2)), dma((nseg, 2)),
                dma((4,)), dma((4,)),
                dma((4,)), dma((4,)),
                dma((4,)), dma((4,)),
                dma((4,)), dma((4,)),
            ],
            compiler_params=pltpu.CompilerParams(
                collective_id=0, has_side_effects=True, vmem_limit_bytes=66400000
            ),
            name="attn",
        )(head_offsets, upstream, out_weight, query_rows, key_rows, value_rows)
        block = jax.ShapeDtypeStruct(query_rows.shape, BF)
        return pl.pallas_call(
            home_kernel,
            out_shape=(block, block, block),
            in_specs=[smem, vmem, vmem, vmem],
            out_specs=(vmem, vmem, vmem),
            name="home",
        )(head_offsets, rkv, rq, rf)

    return jax.shard_map(
        body,
        mesh=mesh,
        in_specs=(
            P(("context", "heads"), None),
            P("heads", None),
            P("context", "heads"),
            P("context", "heads"),
            P("context", "heads"),
            P(),
        ),
        out_specs=(P("context", "heads"), P("context", "heads"), P("context", "heads")),
        check_vma=False,
    )
```

```python
import functools

import jax
import jax.numpy as jnp
from jax import lax
from jax.experimental import pallas as pl
from jax.experimental.pallas import tpu as pltpu
from jax.sharding import PartitionSpec as P

Z = 8
RATE = 16
BF = jnp.bfloat16
F32 = jnp.float32
MESH = pl.DeviceIdType.MESH
LOW = -1e30


def nn(a, b):
    return lax.dot_general(a, b, (((1,), (0,)), ((), ())), preferred_element_type=F32)


def nt(a, b):
    return lax.dot_general(a, b, (((1,), (1,)), ((), ())), preferred_element_type=F32)


def iota(shape, dim):
    return lax.broadcasted_iota(jnp.int32, shape, dim)


def place(rows, offset, zl):
    return 16 * (((rows & 15) - offset + zl + 16) & 15) + (rows >> 4)


def origin(places, offset, zl):
    return 16 * (places & 15) + (((places >> 4) + offset - zl + 16) & 15)


def attn_kernel(
    nseg,
    off_h, up_h, w_h, q_h, k_h, v_h,
    rkv, rq, rf,
    off_ref, w_ref, q_ref, k_ref, v_ref,
    kvs, qts, ots, kv, kt, qt, ot, up, pick, fk, fkt, ex, dp,
    m_s, l_s, f_s, fe, fds, acc_s, fse, fre, sse, sre, rks, rqs, rfs,
    in_s, up_ss, up_rs, qt_ss, qt_rs, kv_ss, kv_rs, fw_ss, ot_ss, ot_rs, pk_ss, pk_rs,
    fa_ss, fa_rs, fb_ss, fb_rs, si_ss, si_rs, rk_ss, rk_rs, rq_ss, rq_rs, rf_ss, rf_rs,
):
    ctx = lax.axis_index("context")
    hd = lax.axis_index("heads")
    s = lax.div(ctx, Z)
    z = lax.rem(ctx, Z)
    xh = lax.div(hd, 2)
    c = lax.rem(hd, 2)
    zh = lax.div(z, 4)
    zl = lax.rem(z, 4)
    oc = 1 - c

    def dev(sv, zv, xv, cv):
        return {"context": sv * Z + zv, "heads": xv * 2 + cv}

    sibling = dev(s, z, xh, oc)
    partner = dev(s, z, 1 - xh, c)

    def peer(i):
        return dev(s, 4 * c + i, xh, zh)

    def far_seg(t):
        return lax.rem(s + t, nseg)

    def is_me(i):
        return jnp.logical_and(zh == c, zl == i)

    def rdma(src, dst, ss, rs, device):
        return pltpu.make_async_remote_copy(
            src_ref=src, dst_ref=dst, send_sem=ss, recv_sem=rs, device_id=device, device_id_type=MESH
        )

    def peer_send(src, dst, ss, rs, i):
        me = is_me(i)

        @pl.when(me)
        def _():
            pltpu.make_async_copy(src, dst, rs).start()

        @pl.when(jnp.logical_not(me))
        def _():
            rdma(src, dst, ss, rs, peer(i)).start()

    def peer_sent(src, ss, i):
        @pl.when(jnp.logical_not(is_me(i)))
        def _():
            rdma(src, src, ss, ss, peer(i)).wait_send()

    def arrived(dst, rs):
        pltpu.make_async_copy(dst, dst, rs).wait()

    code = jnp.where(zl < 2, jnp.where(zl == 0, 228, 225), jnp.where(zl == 2, 54, 27))
    near_last = [lax.rem(lax.div(code, 4**j), 4) for j in range(4)]

    def order_of(half, j):
        return jnp.where(half == zh, near_last[3 - j], near_last[j])

    def order(j):
        return order_of(c, j)

    def step_of(half, j):
        out = order_of(half, 3)
        for n in range(3):
            out = jnp.where(j == n, order_of(half, n), out)
        return out

    bar = pltpu.get_barrier_semaphore()

    def hello(device):
        pl.semaphore_signal(bar, inc=1, device_id=device, device_id_type=MESH)

    for i in range(4):
        @pl.when(jnp.logical_not(is_me(i)))
        def _():
            hello(peer(i))
    hello(sibling)
    hello(partner)
    for t in range(1, nseg):
        for cc in range(2):
            hello(dev(far_seg(t), z, xh, cc))

    loads = [
        pltpu.make_async_copy(a, b, in_s.at[n])
        for n, (a, b) in enumerate(
            ((off_h, off_ref), (q_h, q_ref), (k_h, k_ref), (v_h, v_ref), (up_h, up.at[hd]), (w_h, w_ref))
        )
    ]
    for load in loads:
        load.start()

    for b in range(4):
        qt[b, 64:128, :] = jnp.zeros((64, 256), BF)
        ot[b, 0:64, :] = jnp.zeros((64, 256), BF)
    m_s[...] = jnp.full(m_s.shape, LOW, F32)
    l_s[...] = jnp.zeros(l_s.shape, F32)
    row = iota((1, 256), 1)
    col = iota((256, 256), 0)
    low_half = iota((256, 128), 1) < 64
    lane = iota((1, 128), 1)

    for load in loads[:2]:
        load.wait()
    q_t = q_ref[...].astype(F32).T.astype(BF)
    perms = []
    for h in range(4):
        perm = (col == place(row, off_ref[hd * 4 + h], zl)).astype(F32).astype(BF)
        perms.append(perm)
        qts[h] = (nt(q_t[64 * h : 64 * h + 64, :], perm) * 0.125).astype(BF)
    loads[4].wait()

    pl.semaphore_wait(bar, 4 + 2 + 2 * (nseg - 1) - jnp.where(zh == c, 1, 0))

    rdma(up.at[hd], up.at[hd], up_ss.at[0], up_rs.at[0], partner).start()
    rdma(up.at[hd], up.at[hd], up_ss.at[1], up_rs.at[1], sibling).start()
    for j in range(4):
        i = order(j)
        peer_send(qts.at[i], qt.at[zl, 0:64, :], qt_ss.at[i], qt_rs.at[zl], i)

    for load in loads[2:4]:
        load.wait()
    k_v = [
        jnp.concatenate([k_ref[:, n : n + 128], v_ref[:, n : n + 128]], axis=1) for n in (0, 128)
    ]
    for h in range(4):
        both = nn(perms[h], k_v[h // 2])
        k_p = both[:, 0:128]
        v_p = both[:, 128:256]
        if h % 2:
            k_p = pltpu.roll(k_p, 64, 1)
        else:
            v_p = pltpu.roll(v_p, 64, 1)
        kvs[h] = jnp.where(low_half, k_p, v_p).astype(BF)
    picked = pl.ds(pl.multiple_of(16 * zl, 16), 16)
    for j in range(4):
        i = order(j)
        peer_send(kvs.at[i, picked, :], pick.at[picked, :], pk_ss.at[i], pk_rs.at[zl], i)
    for j in range(4):
        i = order(j)
        peer_send(kvs.at[i], kv.at[z], kv_ss.at[i], kv_rs.at[z], i)

    for i in range(4):
        arrived(pick.at[16 * i : 16 * i + 16, :], pk_rs.at[i])
    for t in range(1, nseg):
        for cc in range(2):
            rdma(
                pick, fk.at[s, c], fa_ss.at[t, cc], fa_rs.at[s, c], dev(far_seg(t), z, xh, cc)
            ).start()
    rdma(pick, fk.at[s, c], fa_ss.at[0, 0], fa_rs.at[s, c], sibling).start()
    fk[s, c] = pick[...]

    far_hd = (1 - xh) * 2 + c
    arrived(up.at[far_hd], up_rs.at[0])
    rdma(up.at[far_hd], up.at[far_hd], up_ss.at[2], up_rs.at[2], sibling).start()
    arrived(up.at[xh * 2 + oc], up_rs.at[1])
    loads[5].wait()
    arrived(up.at[(1 - xh) * 2 + oc], up_rs.at[2])
    a_t = nt(w_ref[...], up[...].reshape(256, up.shape[2])).astype(BF)
    for h in range(4):
        ots[h] = nt(a_t[64 * h : 64 * h + 64, :], perms[h]).astype(BF)
    for j in range(4):
        i = order(j)
        peer_send(ots.at[i], ot.at[zl, 64:128, :], ot_ss.at[i], ot_rs.at[zl], i)

    for i in range(4):
        arrived(qt.at[i, 0:64, :], qt_rs.at[i])

    def score_block(d):
        keys = kv[d]
        kt[d] = keys.astype(F32).T[0:64, :].astype(BF)
        for b in range(4):
            st = nn(keys, qt[b])
            mb = jnp.max(st, axis=0, keepdims=True)
            e = jnp.exp(st - mb)
            ex[d, b] = e
            m_s[b, pl.ds(d, 1), :] = mb
            l_s[b, pl.ds(d, 1), :] = jnp.sum(e, axis=0, keepdims=True)

    def own_block(j, carry):
        i = step_of(c, j)
        d = 4 * c + i
        arrived(kv.at[d], kv_rs.at[d])
        rdma(kv.at[d], kv.at[d], fw_ss.at[i], kv_rs.at[d], sibling).start()
        score_block(d)
        return carry

    def other_block(j, carry):
        d = 4 * oc + step_of(oc, j)
        arrived(kv.at[d], kv_rs.at[d])
        score_block(d)
        return carry

    lax.fori_loop(0, 4, own_block, 0)
    lax.fori_loop(0, 4, other_block, 0)

    def mine(b):
        return jnp.logical_and(lane >= 16 * b, lane < 16 * b + 16)

    def gather_lanes(parts):
        out = jnp.zeros(parts[0].shape, parts[0].dtype)
        for b in range(4):
            out = jnp.where(mine(b), parts[b], out)
        return out

    q_far = gather_lanes([qt[b, :, 0:128].astype(F32) for b in range(4)]).astype(BF)
    for t in range(1, nseg):
        for cc in range(2):
            arrived(fk.at[far_seg(t), cc], fa_rs.at[far_seg(t), cc])
    arrived(fk.at[s, oc], fa_rs.at[s, oc])
    far_keys = fk[...].reshape(nseg * 128, 128)
    fkt[...] = far_keys.astype(F32).T[0:64, :].astype(BF)
    st = nn(far_keys, q_far)
    m_far = jnp.max(st, axis=0, keepdims=True)
    e_far = jnp.exp(st - m_far)
    fe[...] = e_far
    l_far = jnp.sum(e_far, axis=0, keepdims=True)
    for b in range(4):
        m_s[b, Z : Z + 1, 0:128] = jnp.where(mine(b), m_far, LOW)
        l_s[b, Z : Z + 1, 0:128] = jnp.where(mine(b), l_far, 0.0)
    for b in range(4):
        m_all = m_s[b]
        m_row = jnp.max(m_all, axis=0, keepdims=True)
        lse = m_row + jnp.log(jnp.sum(l_s[b] * jnp.exp(m_all - m_row), axis=0, keepdims=True))
        f_s[b] = jnp.exp(m_all - lse)
    fe[...] = fe[...] * gather_lanes([f_s[b, Z : Z + 1, 0:128] for b in range(4)])

    for j in range(4):
        b = order(j)
        arrived(ot.at[b, 64:128, :], ot_rs.at[b])
        o_b = ot[b]

        def dprob_blocks(n, total):
            for m in range(4):
                d = 4 * n + m
                g = nn(kv[d], o_b)
                dp[d, b] = g
                part = jnp.sum(ex[d, b] * g, axis=0, keepdims=True)
                total = total + f_s[b, pl.ds(d, 1), :] * part
            return total

        l_s[b, 0:1, :] = lax.fori_loop(0, 2, dprob_blocks, jnp.zeros((1, 256), F32))

    o_far = gather_lanes([ot[b, :, 0:128].astype(F32) for b in range(4)]).astype(BF)
    g_far = nn(fk[...].reshape(nseg * 128, 128), o_far)
    fds[...] = g_far
    far_delta = jnp.sum(fe[...] * g_far, axis=0, keepdims=True)
    zero_row = jnp.zeros((1, 128), F32)
    delta = [
        l_s[b, 0:1, :] + jnp.concatenate([jnp.where(mine(b), far_delta, 0.0), zero_row], axis=1)
        for b in range(4)
    ]
    for b in range(4):
        l_s[b, 0:1, :] = delta[b]

    for b in range(4):
        acc_s[b] = jnp.zeros((64, 256), F32)

    def grad_block(d):
        key_grads = jnp.zeros((64, 256), F32)
        value_grads = jnp.zeros((64, 256), F32)
        keys_t = kt[d]
        for b in range(4):
            p = ex[d, b] * f_s[b, pl.ds(d, 1), :]
            ds = (p * (dp[d, b] - l_s[b, 0:1, :])).astype(BF)
            key_grads = key_grads + nt(qt[b, 0:64, :], ds)
            value_grads = value_grads + nt(ot[b, 64:128, :], p.astype(BF))
            acc_s[b] = acc_s[b] + nn(keys_t, ds)
        return jnp.concatenate([key_grads, value_grads], axis=0)

    def sibling_block(n):
        i = step_of(oc, n)
        sse[i] = grad_block(4 * oc + i).astype(BF)
        rdma(sse.at[i], sre.at[i], si_ss.at[i], si_rs.at[i], sibling).start()

    def own_grads(n):
        i = step_of(c, n)
        grads = grad_block(4 * c + i)
        arrived(sre.at[i], si_rs.at[i])
        rks[i] = (grads + sre[i].astype(F32)).astype(BF)
        peer_send(rks.at[i], rkv.at[zl], rk_ss.at[i], rk_rs.at[zl], i)

    def pair_block(n, carry):
        sibling_block(n + 1)
        own_grads(n)
        return carry

    sibling_block(0)

    p_far = fe[...]
    ds_far = (p_far * (fds[...] - gather_lanes([delta[b][:, 0:128] for b in range(4)]))).astype(BF)
    dkv_far = nt(ds_far, q_far) + nt(p_far.astype(BF), o_far)
    fse[...] = dkv_far.astype(BF).reshape(nseg, 2, 64, 128)
    for t in range(1, nseg):
        for cc in range(2):
            rdma(
                fse.at[far_seg(t), cc], fre.at[s, c], fb_ss.at[t, cc], fb_rs.at[s, c],
                dev(far_seg(t), z, xh, cc),
            ).start()
    rdma(fse.at[s, oc], fre.at[s, c], fb_ss.at[0, 0], fb_rs.at[s, c], sibling).start()
    fre[s, c] = fse[s, c]
    dq_far = nn(fkt[...], ds_far)
    for b in range(4):
        acc_s[b, :, 0:128] = acc_s[b, :, 0:128] + jnp.where(mine(b), dq_far, 0.0)

    lax.fori_loop(0, 3, pair_block, 0)
    own_grads(3)
    for j in range(4):
        b = order(j)
        rqs[b] = (acc_s[b] * 0.125).astype(BF)
        peer_send(rqs.at[b], rq.at[zl], rq_ss.at[b], rq_rs.at[zl], b)

    for t in range(1, nseg):
        for cc in range(2):
            arrived(fre.at[far_seg(t), cc], fb_rs.at[far_seg(t), cc])
    arrived(fre.at[s, oc], fb_rs.at[s, oc])
    fsum = jnp.zeros((64, 128), F32)
    for t in range(nseg):
        for cc in range(2):
            fsum = fsum + fre[t, cc].astype(F32)
    for i in range(4):
        rfs[i] = fsum[16 * i : 16 * i + 16, :]
    for j in range(4):
        i = order(j)
        peer_send(rfs.at[i], rf.at[zl], rf_ss.at[i], rf_rs.at[zl], i)

    for n, device in ((0, partner), (1, sibling), (2, sibling)):
        rdma(up.at[0], up.at[0], up_ss.at[n], up_ss.at[n], device).wait_send()
    for i in range(4):
        peer_sent(kvs.at[i, 0:16, :], pk_ss.at[i], i)
        peer_sent(qts.at[i], qt_ss.at[i], i)
        peer_sent(kvs.at[i], kv_ss.at[i], i)
        peer_sent(ots.at[i], ot_ss.at[i], i)
        peer_sent(rks.at[i], rk_ss.at[i], i)
        peer_sent(rqs.at[i], rq_ss.at[i], i)
        peer_sent(rfs.at[i], rf_ss.at[i], i)
        rdma(kvs.at[i], kvs.at[i], fw_ss.at[i], fw_ss.at[i], sibling).wait_send()
        rdma(sse.at[i], sse.at[i], si_ss.at[i], si_ss.at[i], sibling).wait_send()
    for t in range(1, nseg):
        for cc in range(2):
            device = dev(far_seg(t), z, xh, cc)
            rdma(pick, pick, fa_ss.at[t, cc], fa_ss.at[t, cc], device).wait_send()
            rdma(pick, pick, fb_ss.at[t, cc], fb_ss.at[t, cc], device).wait_send()
    rdma(pick, pick, fa_ss.at[0, 0], fa_ss.at[0, 0], sibling).wait_send()
    rdma(pick, pick, fb_ss.at[0, 0], fb_ss.at[0, 0], sibling).wait_send()

    for i in range(4):
        arrived(rkv.at[i], rk_rs.at[i])
        arrived(rq.at[i], rq_rs.at[i])
        arrived(rf.at[i], rf_rs.at[i])


def home_kernel(off_ref, rkv, rq, rf, dq_ref, dk_ref, dv_ref):
    ctx = lax.axis_index("context")
    hd = lax.axis_index("heads")
    zl = lax.rem(ctx, 4)
    row = iota((256, 256), 0)
    col = iota((1, 256), 1)
    low_half = iota((256, 128), 1) < 64
    pick = iota((1, 128), 1)
    pick_row = iota((256, 128), 0)
    for pair in range(2):
        lanes = slice(128 * pair, 128 * pair + 128)
        both_q = rq[2 * pair : 2 * pair + 2].reshape(128, 256)
        back, queries = [], []
        for h in (2 * pair, 2 * pair + 1):
            perm = (row == origin(col, off_ref[hd * 4 + h], zl)).astype(F32).astype(BF)
            back_pick = jnp.logical_and(
                pick < 32, pick_row == origin(16 * zl + (pick & 15), off_ref[hd * 4 + h], zl)
            )
            high = rf[h].astype(BF)
            low = (rf[h] - high.astype(F32)).astype(BF)
            far = jnp.concatenate([high, low, jnp.zeros((96, 128), BF)], axis=0)
            back_pick = back_pick.astype(F32).astype(BF)
            back.append(nt(perm, rkv[h]) + nn(back_pick, far))
            queries.append(nt(perm, both_q))
        dq_ref[:, lanes] = jnp.where(low_half, queries[0], queries[1]).astype(BF)
        dk_ref[:, lanes] = jnp.where(low_half, back[0], pltpu.roll(back[1], 64, 1)).astype(BF)
        dv_ref[:, lanes] = jnp.where(low_half, pltpu.roll(back[0], 64, 1), back[1]).astype(BF)


def solution(mesh):
    nseg = mesh.shape["context"] // Z
    vmem = pl.BlockSpec(memory_space=pltpu.VMEM)
    smem = pl.BlockSpec(memory_space=pltpu.SMEM)
    hbm = pl.BlockSpec(memory_space=pltpu.HBM)
    dma = pltpu.SemaphoreType.DMA

    def body(upstream, out_weight, query_rows, key_rows, value_rows, head_offsets):
        width = upstream.shape[1]
        rkv, rq, rf = pl.pallas_call(
            functools.partial(attn_kernel, nseg),
            out_shape=(
                jax.ShapeDtypeStruct((4, 128, 256), BF),
                jax.ShapeDtypeStruct((4, 64, 256), BF),
                jax.ShapeDtypeStruct((4, 16, 128), F32),
            ),
            in_specs=[hbm] * 6,
            out_specs=(hbm, hbm, hbm),
            scratch_shapes=[
                pltpu.SMEM((16,), jnp.int32),
                pltpu.VMEM(out_weight.shape, BF),
                pltpu.VMEM(query_rows.shape, BF),
                pltpu.VMEM(key_rows.shape, BF),
                pltpu.VMEM(value_rows.shape, BF),
                pltpu.VMEM((4, 256, 128), BF),
                pltpu.VMEM((4, 64, 256), BF),
                pltpu.VMEM((4, 64, 256), BF),
                pltpu.VMEM((Z, 256, 128), BF),
                pltpu.VMEM((Z, 64, 256), BF),
                pltpu.VMEM((4, 128, 256), BF),
                pltpu.VMEM((4, 128, 256), BF),
                pltpu.VMEM((4, 64, width), BF),
                pltpu.VMEM((64, 128), BF),
                pltpu.VMEM((nseg, 2, 64, 128), BF),
                pltpu.VMEM((64, nseg * 128), BF),
                pltpu.VMEM((Z, 4, 256, 256), F32),
                pltpu.VMEM((Z, 4, 256, 256), F32),
                pltpu.VMEM((4, 16, 256), F32),
                pltpu.VMEM((4, 16, 256), F32),
                pltpu.VMEM((4, 16, 256), F32),
                pltpu.VMEM((nseg * 128, 128), F32),
                pltpu.VMEM((nseg * 128, 128), F32),
                pltpu.VMEM((4, 64, 256), F32),
                pltpu.VMEM((nseg, 2, 64, 128), BF),
                pltpu.VMEM((nseg, 2, 64, 128), BF),
                pltpu.VMEM((4, 128, 256), BF),
                pltpu.VMEM((4, 128, 256), BF),
                pltpu.VMEM((4, 128, 256), BF),
                pltpu.VMEM((4, 64, 256), BF),
                pltpu.VMEM((4, 16, 128), F32),
                dma((6,)),
                dma((3,)), dma((3,)),
                dma((4,)), dma((4,)),
                dma((4,)), dma((Z,)), dma((4,)),
                dma((4,)), dma((4,)),
                dma((4,)), dma((4,)),
                dma((nseg, 2)), dma((nseg, 2)),
                dma((nseg, 2)), dma((nseg, 2)),
                dma((4,)), dma((4,)),
                dma((4,)), dma((4,)),
                dma((4,)), dma((4,)),
                dma((4,)), dma((4,)),
            ],
            compiler_params=pltpu.CompilerParams(
                collective_id=0, has_side_effects=True, vmem_limit_bytes=66400000
            ),
            name="attn",
        )(head_offsets, upstream, out_weight, query_rows, key_rows, value_rows)
        block = jax.ShapeDtypeStruct(query_rows.shape, BF)
        return pl.pallas_call(
            home_kernel,
            out_shape=(block, block, block),
            in_specs=[smem, vmem, vmem, vmem],
            out_specs=(vmem, vmem, vmem),
            name="home",
        )(head_offsets, rkv, rq, rf)

    return jax.shard_map(
        body,
        mesh=mesh,
        in_specs=(
            P(("context", "heads"), None),
            P("heads", None),
            P("context", "heads"),
            P("context", "heads"),
            P("context", "heads"),
            P(),
        ),
        out_specs=(P("context", "heads"), P("context", "heads"), P("context", "heads")),
        check_vma=False,
    )
```

```python
import functools

import jax
import jax.numpy as jnp
from jax import lax
from jax.experimental import pallas as pl
from jax.experimental.pallas import tpu as pltpu
from jax.sharding import PartitionSpec as P

Z = 8
RATE = 16
BF = jnp.bfloat16
F32 = jnp.float32
MESH = pl.DeviceIdType.MESH
LOW = -1e30


def nn(a, b):
    return lax.dot_general(a, b, (((1,), (0,)), ((), ())), preferred_element_type=F32)


def nt(a, b):
    return lax.dot_general(a, b, (((1,), (1,)), ((), ())), preferred_element_type=F32)


def iota(shape, dim):
    return lax.broadcasted_iota(jnp.int32, shape, dim)


def place(rows, offset, zl):
    return 16 * (((rows & 15) - offset + zl + 16) & 15) + (rows >> 4)


def origin(places, offset, zl):
    return 16 * (places & 15) + (((places >> 4) + offset - zl + 16) & 15)


def attn_kernel(
    nseg,
    off_h, up_h, w_h, q_h, k_h, v_h,
    rkv, rq, rf,
    off_ref, w_ref, q_ref, k_ref, v_ref,
    kvs, qts, ots, kv, kt, qt, ot, up, pick, fk, fkt, ex, dp,
    m_s, l_s, f_s, fe, fds, acc_s, fse, fre, sse, sre, rks, rqs, rfs,
    in_s, up_ss, up_rs, qt_ss, qt_rs, kv_ss, kv_rs, fw_ss, ot_ss, ot_rs, pk_ss, pk_rs,
    fa_ss, fa_rs, fb_ss, fb_rs, si_ss, si_rs, rk_ss, rk_rs, rq_ss, rq_rs, rf_ss, rf_rs,
):
    ctx = lax.axis_index("context")
    hd = lax.axis_index("heads")
    s = lax.div(ctx, Z)
    z = lax.rem(ctx, Z)
    xh = lax.div(hd, 2)
    c = lax.rem(hd, 2)
    zh = lax.div(z, 4)
    zl = lax.rem(z, 4)
    oc = 1 - c

    def dev(sv, zv, xv, cv):
        return {"context": sv * Z + zv, "heads": xv * 2 + cv}

    sibling = dev(s, z, xh, oc)
    partner = dev(s, z, 1 - xh, c)

    def peer(i):
        return dev(s, 4 * c + i, xh, zh)

    def far_seg(t):
        return lax.rem(s + t, nseg)

    def is_me(i):
        return jnp.logical_and(zh == c, zl == i)

    def rdma(src, dst, ss, rs, device):
        return pltpu.make_async_remote_copy(
            src_ref=src, dst_ref=dst, send_sem=ss, recv_sem=rs, device_id=device, device_id_type=MESH
        )

    def peer_send(src, dst, ss, rs, i):
        me = is_me(i)

        @pl.when(me)
        def _():
            pltpu.make_async_copy(src, dst, rs).start()

        @pl.when(jnp.logical_not(me))
        def _():
            rdma(src, dst, ss, rs, peer(i)).start()

    def peer_sent(src, ss, i):
        @pl.when(jnp.logical_not(is_me(i)))
        def _():
            rdma(src, src, ss, ss, peer(i)).wait_send()

    def arrived(dst, rs):
        pltpu.make_async_copy(dst, dst, rs).wait()

    code = jnp.where(zl < 2, jnp.where(zl == 0, 228, 225), jnp.where(zl == 2, 54, 27))
    near_last = [lax.rem(lax.div(code, 4**j), 4) for j in range(4)]

    def order_of(half, j):
        return jnp.where(half == zh, near_last[3 - j], near_last[j])

    def order(j):
        return order_of(c, j)

    def step_of(half, j):
        out = order_of(half, 3)
        for n in range(3):
            out = jnp.where(j == n, order_of(half, n), out)
        return out

    bar = pltpu.get_barrier_semaphore()

    def hello(device):
        pl.semaphore_signal(bar, inc=1, device_id=device, device_id_type=MESH)

    for i in range(4):
        @pl.when(jnp.logical_not(is_me(i)))
        def _():
            hello(peer(i))
    hello(sibling)
    hello(partner)
    for t in range(1, nseg):
        for cc in range(2):
            hello(dev(far_seg(t), z, xh, cc))

    loads = [
        pltpu.make_async_copy(a, b, in_s.at[n])
        for n, (a, b) in enumerate(
            ((off_h, off_ref), (q_h, q_ref), (k_h, k_ref), (v_h, v_ref), (up_h, up.at[hd]), (w_h, w_ref))
        )
    ]
    for load in loads:
        load.start()

    for b in range(4):
        qt[b, 64:128, :] = jnp.zeros((64, 256), BF)
        ot[b, 0:64, :] = jnp.zeros((64, 256), BF)
    m_s[...] = jnp.full(m_s.shape, LOW, F32)
    l_s[...] = jnp.zeros(l_s.shape, F32)
    row = iota((1, 256), 1)
    col = iota((256, 256), 0)
    low_half = iota((256, 128), 1) < 64
    lane = iota((1, 128), 1)

    for load in loads[:2]:
        load.wait()
    q_t = q_ref[...].astype(F32).T.astype(BF)
    perms = []
    for h in range(4):
        perm = (col == place(row, off_ref[hd * 4 + h], zl)).astype(F32).astype(BF)
        perms.append(perm)
        qts[h] = (nt(q_t[64 * h : 64 * h + 64, :], perm) * 0.125).astype(BF)
    loads[4].wait()

    pl.semaphore_wait(bar, 4 + 2 + 2 * (nseg - 1) - jnp.where(zh == c, 1, 0))

    rdma(up.at[hd], up.at[hd], up_ss.at[0], up_rs.at[0], partner).start()
    rdma(up.at[hd], up.at[hd], up_ss.at[1], up_rs.at[1], sibling).start()
    for j in range(4):
        i = order(j)
        peer_send(qts.at[i], qt.at[zl, 0:64, :], qt_ss.at[i], qt_rs.at[zl], i)

    for load in loads[2:4]:
        load.wait()
    k_v = [
        jnp.concatenate([k_ref[:, n : n + 128], v_ref[:, n : n + 128]], axis=1) for n in (0, 128)
    ]
    for h in range(4):
        both = nn(perms[h], k_v[h // 2])
        k_p = both[:, 0:128]
        v_p = both[:, 128:256]
        if h % 2:
            k_p = pltpu.roll(k_p, 64, 1)
        else:
            v_p = pltpu.roll(v_p, 64, 1)
        kvs[h] = jnp.where(low_half, k_p, v_p).astype(BF)
    picked = pl.ds(pl.multiple_of(16 * zl, 16), 16)
    for j in range(4):
        i = order(j)
        peer_send(kvs.at[i, picked, :], pick.at[picked, :], pk_ss.at[i], pk_rs.at[zl], i)
    for j in range(4):
        i = order(j)
        peer_send(kvs.at[i], kv.at[z], kv_ss.at[i], kv_rs.at[z], i)

    for i in range(4):
        arrived(pick.at[16 * i : 16 * i + 16, :], pk_rs.at[i])
    for t in range(1, nseg):
        for cc in range(2):
            rdma(
                pick, fk.at[s, c], fa_ss.at[t, cc], fa_rs.at[s, c], dev(far_seg(t), z, xh, cc)
            ).start()
    rdma(pick, fk.at[s, c], fa_ss.at[0, 0], fa_rs.at[s, c], sibling).start()
    fk[s, c] = pick[...]

    far_hd = (1 - xh) * 2 + c
    arrived(up.at[far_hd], up_rs.at[0])
    rdma(up.at[far_hd], up.at[far_hd], up_ss.at[2], up_rs.at[2], sibling).start()
    arrived(up.at[xh * 2 + oc], up_rs.at[1])
    loads[5].wait()
    arrived(up.at[(1 - xh) * 2 + oc], up_rs.at[2])
    a_t = nt(w_ref[...], up[...].reshape(256, up.shape[2])).astype(BF)
    for h in range(4):
        ots[h] = nt(a_t[64 * h : 64 * h + 64, :], perms[h]).astype(BF)
    for j in range(4):
        i = order(j)
        peer_send(ots.at[i], ot.at[zl, 64:128, :], ot_ss.at[i], ot_rs.at[zl], i)

    for i in range(4):
        arrived(qt.at[i, 0:64, :], qt_rs.at[i])

    def score_block(d):
        keys = kv[d]
        kt[d] = keys.astype(F32).T[0:64, :].astype(BF)
        for b in range(4):
            st = nn(keys, qt[b])
            mb = jnp.max(st, axis=0, keepdims=True)
            e = jnp.exp(st - mb)
            ex[d, b] = e
            m_s[b, pl.ds(d, 1), :] = mb
            l_s[b, pl.ds(d, 1), :] = jnp.sum(e, axis=0, keepdims=True)

    def own_block(j, carry):
        i = step_of(c, j)
        d = 4 * c + i
        arrived(kv.at[d], kv_rs.at[d])
        rdma(kv.at[d], kv.at[d], fw_ss.at[i], kv_rs.at[d], sibling).start()
        score_block(d)
        return carry

    def other_block(j, carry):
        d = 4 * oc + step_of(oc, j)
        arrived(kv.at[d], kv_rs.at[d])
        score_block(d)
        return carry

    lax.fori_loop(0, 4, own_block, 0)
    lax.fori_loop(0, 4, other_block, 0)

    def mine(b):
        return jnp.logical_and(lane >= 16 * b, lane < 16 * b + 16)

    def gather_lanes(parts):
        out = jnp.zeros(parts[0].shape, parts[0].dtype)
        for b in range(4):
            out = jnp.where(mine(b), parts[b], out)
        return out

    q_far = gather_lanes([qt[b, :, 0:128].astype(F32) for b in range(4)]).astype(BF)
    for t in range(1, nseg):
        for cc in range(2):
            arrived(fk.at[far_seg(t), cc], fa_rs.at[far_seg(t), cc])
    arrived(fk.at[s, oc], fa_rs.at[s, oc])
    far_keys = fk[...].reshape(nseg * 128, 128)
    fkt[...] = far_keys.astype(F32).T[0:64, :].astype(BF)
    st = nn(far_keys, q_far)
    m_far = jnp.max(st, axis=0, keepdims=True)
    e_far = jnp.exp(st - m_far)
    fe[...] = e_far
    l_far = jnp.sum(e_far, axis=0, keepdims=True)
    for b in range(4):
        m_s[b, Z : Z + 1, 0:128] = jnp.where(mine(b), m_far, LOW)
        l_s[b, Z : Z + 1, 0:128] = jnp.where(mine(b), l_far, 0.0)
    for b in range(4):
        m_all = m_s[b]
        m_row = jnp.max(m_all, axis=0, keepdims=True)
        lse = m_row + jnp.log(jnp.sum(l_s[b] * jnp.exp(m_all - m_row), axis=0, keepdims=True))
        f_s[b] = jnp.exp(m_all - lse)
    fe[...] = fe[...] * gather_lanes([f_s[b, Z : Z + 1, 0:128] for b in range(4)])

    for j in range(4):
        b = order(j)
        arrived(ot.at[b, 64:128, :], ot_rs.at[b])
        o_b = ot[b]

        def dprob_blocks(n, total):
            for m in range(4):
                d = 4 * n + m
                g = nn(kv[d], o_b)
                dp[d, b] = g
                part = jnp.sum(ex[d, b] * g, axis=0, keepdims=True)
                total = total + f_s[b, pl.ds(d, 1), :] * part
            return total

        l_s[b, 0:1, :] = lax.fori_loop(0, 2, dprob_blocks, jnp.zeros((1, 256), F32))

    o_far = gather_lanes([ot[b, :, 0:128].astype(F32) for b in range(4)]).astype(BF)
    g_far = nn(fk[...].reshape(nseg * 128, 128), o_far)
    fds[...] = g_far
    far_delta = jnp.sum(fe[...] * g_far, axis=0, keepdims=True)
    zero_row = jnp.zeros((1, 128), F32)
    delta = [
        l_s[b, 0:1, :] + jnp.concatenate([jnp.where(mine(b), far_delta, 0.0), zero_row], axis=1)
        for b in range(4)
    ]
    for b in range(4):
        l_s[b, 0:1, :] = delta[b]

    for b in range(4):
        acc_s[b] = jnp.zeros((64, 256), F32)

    def grad_block(d):
        key_grads = jnp.zeros((64, 256), F32)
        value_grads = jnp.zeros((64, 256), F32)
        keys_t = kt[d]
        for b in range(4):
            p = ex[d, b] * f_s[b, pl.ds(d, 1), :]
            ds = (p * (dp[d, b] - l_s[b, 0:1, :])).astype(BF)
            key_grads = key_grads + nt(qt[b, 0:64, :], ds)
            value_grads = value_grads + nt(ot[b, 64:128, :], p.astype(BF))
            acc_s[b] = acc_s[b] + nn(keys_t, ds)
        return jnp.concatenate([key_grads, value_grads], axis=0)

    def sibling_block(n):
        i = step_of(oc, n)
        sse[i] = grad_block(4 * oc + i).astype(BF)
        rdma(sse.at[i], sre.at[i], si_ss.at[i], si_rs.at[i], sibling).start()

    def own_grads(n):
        i = step_of(c, n)
        grads = grad_block(4 * c + i)
        arrived(sre.at[i], si_rs.at[i])
        rks[i] = (grads + sre[i].astype(F32)).astype(BF)
        peer_send(rks.at[i], rkv.at[zl], rk_ss.at[i], rk_rs.at[zl], i)

    def pair_block(n, carry):
        sibling_block(n + 1)
        own_grads(n)
        return carry

    sibling_block(0)

    p_far = fe[...]
    ds_far = (p_far * (fds[...] - gather_lanes([delta[b][:, 0:128] for b in range(4)]))).astype(BF)
    dkv_far = nt(ds_far, q_far) + nt(p_far.astype(BF), o_far)
    fse[...] = dkv_far.astype(BF).reshape(nseg, 2, 64, 128)
    for t in range(1, nseg):
        for cc in range(2):
            rdma(
                fse.at[far_seg(t), cc], fre.at[s, c], fb_ss.at[t, cc], fb_rs.at[s, c],
                dev(far_seg(t), z, xh, cc),
            ).start()
    rdma(fse.at[s, oc], fre.at[s, c], fb_ss.at[0, 0], fb_rs.at[s, c], sibling).start()
    fre[s, c] = fse[s, c]
    dq_far = nn(fkt[...], ds_far)
    for b in range(4):
        acc_s[b, :, 0:128] = acc_s[b, :, 0:128] + jnp.where(mine(b), dq_far, 0.0)

    own_grads(0)
    sibling_block(1)
    lax.fori_loop(1, 3, pair_block, 0)
    own_grads(3)
    for j in range(4):
        b = order(j)
        rqs[b] = (acc_s[b] * 0.125).astype(BF)
        peer_send(rqs.at[b], rq.at[zl], rq_ss.at[b], rq_rs.at[zl], b)

    for t in range(1, nseg):
        for cc in range(2):
            arrived(fre.at[far_seg(t), cc], fb_rs.at[far_seg(t), cc])
    arrived(fre.at[s, oc], fb_rs.at[s, oc])
    fsum = jnp.zeros((64, 128), F32)
    for t in range(nseg):
        for cc in range(2):
            fsum = fsum + fre[t, cc].astype(F32)
    for i in range(4):
        rfs[i] = fsum[16 * i : 16 * i + 16, :]
    for j in range(4):
        i = order(j)
        peer_send(rfs.at[i], rf.at[zl], rf_ss.at[i], rf_rs.at[zl], i)

    for n, device in ((0, partner), (1, sibling), (2, sibling)):
        rdma(up.at[0], up.at[0], up_ss.at[n], up_ss.at[n], device).wait_send()
    for i in range(4):
        peer_sent(kvs.at[i, 0:16, :], pk_ss.at[i], i)
        peer_sent(qts.at[i], qt_ss.at[i], i)
        peer_sent(kvs.at[i], kv_ss.at[i], i)
        peer_sent(ots.at[i], ot_ss.at[i], i)
        peer_sent(rks.at[i], rk_ss.at[i], i)
        peer_sent(rqs.at[i], rq_ss.at[i], i)
        peer_sent(rfs.at[i], rf_ss.at[i], i)
        rdma(kvs.at[i], kvs.at[i], fw_ss.at[i], fw_ss.at[i], sibling).wait_send()
        rdma(sse.at[i], sse.at[i], si_ss.at[i], si_ss.at[i], sibling).wait_send()
    for t in range(1, nseg):
        for cc in range(2):
            device = dev(far_seg(t), z, xh, cc)
            rdma(pick, pick, fa_ss.at[t, cc], fa_ss.at[t, cc], device).wait_send()
            rdma(pick, pick, fb_ss.at[t, cc], fb_ss.at[t, cc], device).wait_send()
    rdma(pick, pick, fa_ss.at[0, 0], fa_ss.at[0, 0], sibling).wait_send()
    rdma(pick, pick, fb_ss.at[0, 0], fb_ss.at[0, 0], sibling).wait_send()

    for i in range(4):
        arrived(rkv.at[i], rk_rs.at[i])
        arrived(rq.at[i], rq_rs.at[i])
        arrived(rf.at[i], rf_rs.at[i])


def home_kernel(off_ref, rkv, rq, rf, dq_ref, dk_ref, dv_ref):
    ctx = lax.axis_index("context")
    hd = lax.axis_index("heads")
    zl = lax.rem(ctx, 4)
    row = iota((256, 256), 0)
    col = iota((1, 256), 1)
    low_half = iota((256, 128), 1) < 64
    pick = iota((1, 128), 1)
    pick_row = iota((256, 128), 0)
    for pair in range(2):
        lanes = slice(128 * pair, 128 * pair + 128)
        both_q = rq[2 * pair : 2 * pair + 2].reshape(128, 256)
        back, queries = [], []
        for h in (2 * pair, 2 * pair + 1):
            perm = (row == origin(col, off_ref[hd * 4 + h], zl)).astype(F32).astype(BF)
            back_pick = jnp.logical_and(
                pick < 32, pick_row == origin(16 * zl + (pick & 15), off_ref[hd * 4 + h], zl)
            )
            high = rf[h].astype(BF)
            low = (rf[h] - high.astype(F32)).astype(BF)
            far = jnp.concatenate([high, low, jnp.zeros((96, 128), BF)], axis=0)
            back_pick = back_pick.astype(F32).astype(BF)
            back.append(nt(perm, rkv[h]) + nn(back_pick, far))
            queries.append(nt(perm, both_q))
        dq_ref[:, lanes] = jnp.where(low_half, queries[0], queries[1]).astype(BF)
        dk_ref[:, lanes] = jnp.where(low_half, back[0], pltpu.roll(back[1], 64, 1)).astype(BF)
        dv_ref[:, lanes] = jnp.where(low_half, pltpu.roll(back[0], 64, 1), back[1]).astype(BF)


def solution(mesh):
    nseg = mesh.shape["context"] // Z
    vmem = pl.BlockSpec(memory_space=pltpu.VMEM)
    smem = pl.BlockSpec(memory_space=pltpu.SMEM)
    hbm = pl.BlockSpec(memory_space=pltpu.HBM)
    dma = pltpu.SemaphoreType.DMA

    def body(upstream, out_weight, query_rows, key_rows, value_rows, head_offsets):
        width = upstream.shape[1]
        rkv, rq, rf = pl.pallas_call(
            functools.partial(attn_kernel, nseg),
            out_shape=(
                jax.ShapeDtypeStruct((4, 128, 256), BF),
                jax.ShapeDtypeStruct((4, 64, 256), BF),
                jax.ShapeDtypeStruct((4, 16, 128), F32),
            ),
            in_specs=[hbm] * 6,
            out_specs=(hbm, hbm, hbm),
            scratch_shapes=[
                pltpu.SMEM((16,), jnp.int32),
                pltpu.VMEM(out_weight.shape, BF),
                pltpu.VMEM(query_rows.shape, BF),
                pltpu.VMEM(key_rows.shape, BF),
                pltpu.VMEM(value_rows.shape, BF),
                pltpu.VMEM((4, 256, 128), BF),
                pltpu.VMEM((4, 64, 256), BF),
                pltpu.VMEM((4, 64, 256), BF),
                pltpu.VMEM((Z, 256, 128), BF),
                pltpu.VMEM((Z, 64, 256), BF),
                pltpu.VMEM((4, 128, 256), BF),
                pltpu.VMEM((4, 128, 256), BF),
                pltpu.VMEM((4, 64, width), BF),
                pltpu.VMEM((64, 128), BF),
                pltpu.VMEM((nseg, 2, 64, 128), BF),
                pltpu.VMEM((64, nseg * 128), BF),
                pltpu.VMEM((Z, 4, 256, 256), F32),
                pltpu.VMEM((Z, 4, 256, 256), F32),
                pltpu.VMEM((4, 16, 256), F32),
                pltpu.VMEM((4, 16, 256), F32),
                pltpu.VMEM((4, 16, 256), F32),
                pltpu.VMEM((nseg * 128, 128), F32),
                pltpu.VMEM((nseg * 128, 128), F32),
                pltpu.VMEM((4, 64, 256), F32),
                pltpu.VMEM((nseg, 2, 64, 128), BF),
                pltpu.VMEM((nseg, 2, 64, 128), BF),
                pltpu.VMEM((4, 128, 256), BF),
                pltpu.VMEM((4, 128, 256), BF),
                pltpu.VMEM((4, 128, 256), BF),
                pltpu.VMEM((4, 64, 256), BF),
                pltpu.VMEM((4, 16, 128), F32),
                dma((6,)),
                dma((3,)), dma((3,)),
                dma((4,)), dma((4,)),
                dma((4,)), dma((Z,)), dma((4,)),
                dma((4,)), dma((4,)),
                dma((4,)), dma((4,)),
                dma((nseg, 2)), dma((nseg, 2)),
                dma((nseg, 2)), dma((nseg, 2)),
                dma((4,)), dma((4,)),
                dma((4,)), dma((4,)),
                dma((4,)), dma((4,)),
                dma((4,)), dma((4,)),
            ],
            compiler_params=pltpu.CompilerParams(
                collective_id=0, has_side_effects=True, vmem_limit_bytes=66400000
            ),
            name="attn",
        )(head_offsets, upstream, out_weight, query_rows, key_rows, value_rows)
        block = jax.ShapeDtypeStruct(query_rows.shape, BF)
        return pl.pallas_call(
            home_kernel,
            out_shape=(block, block, block),
            in_specs=[smem, vmem, vmem, vmem],
            out_specs=(vmem, vmem, vmem),
            name="home",
        )(head_offsets, rkv, rq, rf)

    return jax.shard_map(
        body,
        mesh=mesh,
        in_specs=(
            P(("context", "heads"), None),
            P("heads", None),
            P("context", "heads"),
            P("context", "heads"),
            P("context", "heads"),
            P(),
        ),
        out_specs=(P("context", "heads"), P("context", "heads"), P("context", "heads")),
        check_vma=False,
    )
```
